512 devices in a mesh: ctx: 32 (over x, z_lo), tp: 16 (over y, z_hi, core).
Axes of the slice: x: 4, y: 4, z: 16 (z_hi: 2, z_lo: 8; z = z_hi * 8 + z_lo), core: 2. Of those that a mesh axis runs over, the one named last changes fastest.
Arguments:
- queries: bfloat16 [4096, 4096], P('ctx', 'tp'), may hold values from -5 to 5
- key_states: bfloat16 [4096, 4096], P('ctx', 'tp'), may hold values from -5 to 5
- value_states: bfloat16 [4096, 4096], P('ctx', 'tp'), may hold values from -6 to 6
- attn_output: bfloat16 [4096, 4096], P('ctx', 'tp'), may hold values from -6 to 6
- output_grad: bfloat16 [4096, 4096], P('ctx', 'tp'), may hold values from -6 to 6
- block_map: int32 [32, 32], replicated, may hold values from 0 to 1, as said below
- w_query: bfloat16 [8192, 4096], P('ctx', 'tp'), may hold values from -0.09375 to 0.09375
- w_key: bfloat16 [8192, 4096], P('ctx', 'tp'), may hold values from -0.09375 to 0.09375
- w_value: bfloat16 [8192, 4096], P('ctx', 'tp'), may hold values from -0.09375 to 0.09375
Outputs:
- grad_input: bfloat16 [4096, 8192], P('tp', 'ctx')
The draws below stay inside these ranges and needn't reach their ends.
Inputs may be any that keep to these rules, and one draw needn't show every extreme that they name: block_map[i, j] is 1 wherever |i - j| <= 1; elsewhere each row is 1 on a share of its entries that differs from row to row.
All inputs are finite; a program needn't handle non-finite values.
Results may differ from the reference program's by a relative error of at most 0.014.
Values may be sent and summed in bfloat16 or wider, within the bound.
No kernel may reach another device: no remote copies, remote signals or barrier semaphores. Data moves between devices by JAX's collectives and lax.ppermute only.
A program may use at most 64 MiB of HBM per device.

```python
import math
import jax
import jax.numpy as jnp
from jax import lax

D = 8192
HD = 128
HEADS_DEV = 2
BLK = 128
SLAB = 128
TOKENS = 4096
HEADS = 32
HC = 4096
N_CTX = 32
N_TP = 16


def draw_queries(key, part):
    base = jnp.clip(jax.random.normal(jax.random.fold_in(key, 1), (TOKENS, HC), jnp.float32), -5.0, 5.0)
    return base.astype(jnp.bfloat16)


def draw_key_states(key, part):
    base = jnp.clip(jax.random.normal(jax.random.fold_in(key, 2), (TOKENS, HC), jnp.float32), -5.0, 5.0)
    return base.astype(jnp.bfloat16)


def draw_block_map(key, part):
    count = TOKENS // BLK
    density = jax.random.randint(jax.random.fold_in(key, 5), (count, 1), 1, 16)
    coins = jax.random.randint(jax.random.fold_in(key, 6), (count, count), 0, 16)
    rows = jnp.arange(count)
    near = jnp.abs(rows[:, None] - rows[None, :]) <= 1
    return jnp.where(near | (coins < density), 1, 0).astype(jnp.int32)


def levels(key, shape, split, smallest, largest):
    def one(axis_at, blocks):
        heights = jax.random.uniform(jax.random.fold_in(jax.random.fold_in(key, 6), axis_at), (blocks,), jnp.float32, smallest / len(split), largest / len(split))
        return jnp.repeat(jnp.exp(heights), shape[axis_at] // blocks).reshape((-1,) + (1,) * (len(shape) - axis_at - 1))

    level = one(*split[0])
    for cut in split[1:]:
        level = level * one(*cut)
    return level


def normal_values(own_key, shape, scale, most, shards=(), held_as=jnp.bfloat16):
    entries = jax.random.normal(own_key, shape, jnp.float32) * scale
    if len(shards) > 0:
        entries = levels(own_key, shape, shards, -0.22, 0.18) * entries
    return jnp.clip(entries, min=-most, max=most).astype(held_as)


def setup_inputs(seed: int = 0) -> dict:
    seeds = jax.random.split(jax.random.key(seed), 10)
    return {
        "queries": draw_queries(jax.random.fold_in(seeds[9], 71), 0),
        "key_states": draw_key_states(jax.random.fold_in(seeds[9], 71), 0),
        "value_states": normal_values(seeds[2], (TOKENS, HC), 1.0, 6.0, ((0, 32), (1, 16))),
        "attn_output": normal_values(seeds[3], (TOKENS, HC), 1.0, 6.0, ((0, 32), (1, 16))),
        "output_grad": normal_values(seeds[4], (TOKENS, HC), 1.0, 6.0, ((0, 32), (1, 16))),
        "block_map": draw_block_map(jax.random.fold_in(seeds[9], 71), 0),
        "w_query": normal_values(seeds[6], (D, HC), HC ** -0.5, 0.09375, ((0, 32), (1, 16))),
        "w_key": normal_values(seeds[7], (D, HC), HC ** -0.5, 0.09375, ((0, 32), (1, 16))),
        "w_value": normal_values(seeds[8], (D, HC), HC ** -0.5, 0.09375, ((0, 32), (1, 16))),
    }


NEG_FILL = -1e+30

def expand_map(block_map):
    count = block_map.shape[0]
    spread = jnp.broadcast_to(block_map[:, None, :, None], (count, BLK, count, BLK))
    return spread.reshape(count * BLK, count * BLK) > 0

def resolved_rows(values):
    return lax.optimization_barrier(values.astype(jnp.bfloat16)).astype(jnp.float32)

def head_grads(head_index, queries, key_states, value_states, attn_output, output_grad, allowed):

    def columns(array):
        return lax.dynamic_slice_in_dim(array, head_index * HD, HD, 1)
    query_head = columns(queries)
    key_head_index = columns(key_states)
    value_head = columns(value_states)
    output_head = columns(attn_output)
    grad_head = columns(output_grad)
    score_scale = 1.0 / math.sqrt(HD)
    scores = jnp.dot(query_head, key_head_index.T, preferred_element_type=jnp.float32) * score_scale
    masked = jnp.where(allowed, scores, NEG_FILL)
    row_max = lax.optimization_barrier(jnp.max(masked, axis=1, keepdims=True))
    row_sum = lax.optimization_barrier(jnp.sum(jnp.where(allowed, jnp.exp(masked - row_max), 0.0), axis=1, keepdims=True))
    log_total = row_max + jnp.log(row_sum)
    probs = jnp.where(allowed, jnp.exp(masked - log_total), 0.0)
    probs_low = probs.astype(jnp.bfloat16)
    dprobs = jnp.dot(grad_head, value_head.T, preferred_element_type=jnp.float32)
    row_delta = lax.optimization_barrier(jnp.sum(grad_head.astype(jnp.float32) * output_head.astype(jnp.float32), axis=1, keepdims=True))
    score_gradient = (probs * (dprobs - row_delta) * score_scale).astype(jnp.bfloat16)

    def split_rows(matrix):
        return matrix.astype(jnp.float32).reshape(N_CTX, SLAB, N_CTX, SLAB)

    def rows_for_part(array):
        return array.astype(jnp.float32).reshape(N_CTX, SLAB, HD)
    grad_v = lax.optimization_barrier(jnp.sum(resolved_rows(jnp.einsum('aqbk,aqd->abkd', split_rows(probs_low), rows_for_part(grad_head))), axis=0))
    grad_k = lax.optimization_barrier(jnp.sum(resolved_rows(jnp.einsum('aqbk,aqd->abkd', split_rows(score_gradient), rows_for_part(query_head))), axis=0))
    query_gradient = lax.optimization_barrier(jnp.sum(resolved_rows(jnp.einsum('hpru,rug->hrpg', split_rows(score_gradient), rows_for_part(key_head_index))), axis=1))
    return (query_gradient.reshape(TOKENS, HD).astype(jnp.bfloat16), grad_k.reshape(TOKENS, HD).astype(jnp.bfloat16), grad_v.reshape(TOKENS, HD).astype(jnp.bfloat16))

def reference(queries, key_states, value_states, attn_output, output_grad, block_map, w_query, w_key, w_value):
    allowed = expand_map(block_map)

    def one_head(head_index):
        return head_grads(head_index, queries, key_states, value_states, attn_output, output_grad, allowed)
    query_gradient, grad_k, grad_v = lax.map(one_head, jnp.arange(HEADS, dtype=jnp.int32))

    def joined(stack):
        return jnp.transpose(stack, (1, 0, 2)).reshape(TOKENS, HEADS * HD)
    query_gradient, grad_k, grad_v = (joined(query_gradient), joined(grad_k), joined(grad_v))
    group_width = HEADS_DEV * HD

    def group_step(summed, group_index):

        def columns(array):
            return lax.dynamic_slice_in_dim(array, group_index * group_width, group_width, 1)
        term = jnp.dot(columns(query_gradient), columns(w_query).T, preferred_element_type=jnp.float32)
        term = term + jnp.dot(columns(grad_k), columns(w_key).T, preferred_element_type=jnp.float32)
        term = term + jnp.dot(columns(grad_v), columns(w_value).T, preferred_element_type=jnp.float32)
        return (summed + resolved_rows(term), None)
    summed, _ = lax.scan(group_step, jnp.zeros((TOKENS, D), jnp.float32), jnp.arange(N_TP, dtype=jnp.int32))
    return summed.astype(jnp.bfloat16)
```

```python
import math

import jax
import jax.numpy as jnp
from jax import lax
from jax.sharding import PartitionSpec as P

HD = 128
BLK = 128


NEG_FILL = -1e30


def block_mask(block_map, row_offset, row_count, col_offset, col_count):
    tiles = lax.dynamic_slice(
        block_map, (row_offset // BLK, col_offset // BLK), (row_count // BLK, col_count // BLK)
    )
    spread = jnp.broadcast_to(
        tiles[:, None, :, None], (row_count // BLK, BLK, col_count // BLK, BLK)
    )
    return spread.reshape(row_count, col_count) > 0


def resolved_rows(values):
    return lax.optimization_barrier(values.astype(jnp.bfloat16)).astype(jnp.float32)


def stat_update(state, query_heads, key_block, allowed, score_scale):
    row_max, row_sum = state
    scores = (
        jnp.einsum("qhd,khd->hqk", query_heads, key_block, preferred_element_type=jnp.float32)
        * score_scale
    )
    masked = jnp.where(allowed[None], scores, NEG_FILL)
    new_max = jnp.maximum(row_max, jnp.max(masked, axis=2))
    kept = jnp.where(allowed[None], jnp.exp(masked - new_max[:, :, None]), 0.0)
    return (new_max, row_sum * jnp.exp(row_max - new_max) + jnp.sum(kept, axis=2))


def gradient_block(
    query_heads, grad_heads, key_block, value_block, log_total, row_delta, allowed, score_scale
):
    scores = (
        jnp.einsum("qhd,khd->hqk", query_heads, key_block, preferred_element_type=jnp.float32)
        * score_scale
    )
    masked = jnp.where(allowed[None], scores, NEG_FILL)
    probs = jnp.where(allowed[None], jnp.exp(masked - log_total[:, :, None]), 0.0)
    probs_low = probs.astype(jnp.bfloat16)
    dprobs = jnp.einsum("qhd,khd->hqk", grad_heads, value_block, preferred_element_type=jnp.float32)
    score_gradient = (probs * (dprobs - row_delta[:, :, None]) * score_scale).astype(jnp.bfloat16)
    return (probs_low, score_gradient)


def per_device(
    queries, key_states, value_states, attn_output, output_grad, block_map, w_query, w_key, w_value
):
    slab_rows, width = queries.shape
    head_count = width // HD
    context_count = lax.axis_size("ctx")
    score_scale = 1.0 / math.sqrt(HD)
    row_offset = lax.axis_index("ctx") * slab_rows
    query_heads = queries.reshape(slab_rows, head_count, HD)
    grad_heads = output_grad.reshape(slab_rows, head_count, HD)
    output_heads = attn_output.reshape(slab_rows, head_count, HD)
    row_delta = jnp.sum(grad_heads.astype(jnp.float32) * output_heads.astype(jnp.float32), axis=2).T
    start_state = (
        jnp.full((head_count, slab_rows), NEG_FILL, jnp.float32),
        jnp.zeros((head_count, slab_rows), jnp.float32),
    )
    key_value = jnp.concatenate([key_states, value_states], axis=1)
    spread = jnp.broadcast_to(key_value[None], (context_count,) + key_value.shape)
    gathered = lax.all_to_all(spread, "ctx", 0, 0, tiled=True).reshape(
        context_count * slab_rows, 2 * width
    )
    full_keys, full_values = gathered[:, :width], gathered[:, width:]
    group_size = min(context_count, max(1, 512 // slab_rows))
    key_span = slab_rows * group_size
    total_block_count = context_count // group_size
    key_blocks = full_keys.reshape(total_block_count, key_span, head_count, HD)
    value_blocks = full_values.reshape(total_block_count, key_span, head_count, HD)
    block_ids = jnp.arange(total_block_count, dtype=jnp.int32)

    def stat_step(state, inputs):
        key_block, block_index = inputs
        allowed = block_mask(block_map, row_offset, slab_rows, block_index * key_span, key_span)

        def stat_active_step(previous):
            return stat_update(previous, query_heads, key_block, allowed, score_scale)

        return (
            lax.cond(jnp.any(allowed), stat_active_step, lambda previous: previous, state),
            None,
        )

    (row_max, row_sum), _ = lax.scan(stat_step, start_state, (key_blocks, block_ids))
    log_total = row_max + jnp.log(row_sum)

    def back_step(dq_total, inputs):
        key_block, value_block, block_index = inputs
        allowed = block_mask(block_map, row_offset, slab_rows, block_index * key_span, key_span)

        def back_active_step(previous):
            probs_low, score_gradient = gradient_block(
                query_heads,
                grad_heads,
                key_block,
                value_block,
                log_total,
                row_delta,
                allowed,
                score_scale,
            )
            dv_part = jnp.einsum(
                "hqk,qhd->khd", probs_low, grad_heads, preferred_element_type=jnp.float32
            ).astype(jnp.bfloat16)
            dk_part = jnp.einsum(
                "hqk,qhd->khd", score_gradient, query_heads, preferred_element_type=jnp.float32
            ).astype(jnp.bfloat16)
            per_slab = jnp.einsum(
                "hqgk,gkhd->gqhd",
                score_gradient.reshape(head_count, slab_rows, group_size, slab_rows),
                key_block.reshape(group_size, slab_rows, head_count, HD),
                preferred_element_type=jnp.float32,
            )
            joined = jnp.concatenate(
                [dk_part.reshape(key_span, width), dv_part.reshape(key_span, width)], axis=1
            )
            return (previous + jnp.sum(resolved_rows(per_slab), axis=0), joined)

        def empty_step(previous):
            return (previous, jnp.zeros((key_span, 2 * width), jnp.bfloat16))

        return lax.cond(jnp.any(allowed), back_active_step, empty_step, dq_total)

    dq_total, joined_blocks = lax.scan(
        back_step,
        jnp.zeros((slab_rows, head_count, HD), jnp.float32),
        (key_blocks, value_blocks, block_ids),
    )
    local_grads = dq_total.astype(jnp.bfloat16).reshape(slab_rows, width)
    part_grads = joined_blocks.reshape(context_count * slab_rows, 2 * width)
    part_width = part_grads.shape[1]
    arrived = lax.all_to_all(
        part_grads.reshape(context_count, slab_rows, part_width),
        "ctx",
        split_axis=0,
        concat_axis=0,
        tiled=True,
    )
    finished = jnp.sum(arrived.astype(jnp.float32), axis=0).astype(jnp.bfloat16)
    own_grads = jnp.concatenate([local_grads, finished], axis=1)
    gradients = lax.all_gather(own_grads, "ctx", axis=0, tiled=True)
    projections = jnp.concatenate([w_query, w_key, w_value], axis=1)
    return lax.psum_scatter(
        lax.dot_general(
            gradients, projections, (((1,), (1,)), ((), ())), preferred_element_type=jnp.float32
        ).astype(jnp.bfloat16),
        "tp",
        scatter_dimension=0,
        tiled=True,
    )


def solution(mesh):
    return jax.shard_map(
        per_device,
        mesh=mesh,
        in_specs=(
            P("ctx", "tp"),
            P("ctx", "tp"),
            P("ctx", "tp"),
            P("ctx", "tp"),
            P("ctx", "tp"),
            P(),
            P("ctx", "tp"),
            P("ctx", "tp"),
            P("ctx", "tp"),
        ),
        out_specs=P("tp", "ctx"),
        check_vma=False,
    )
```

```python
import functools
import math

import jax
import jax.numpy as jnp
from jax import lax
from jax.experimental import pallas as pl
from jax.experimental.pallas import tpu as pltpu
from jax.sharding import PartitionSpec as P

HD = 128
BLK = 128


NEG_FILL = -1e30


def _nt(a, b):
    return lax.dot_general(a, b, (((1,), (1,)), ((), ())), preferred_element_type=jnp.float32)


def _tn(a, b):
    return lax.dot_general(a, b, (((0,), (0,)), ((), ())), preferred_element_type=jnp.float32)


def attention_kernel(
    head_count, block_count, score_scale,
    row_map, q_ref, do_ref, o_ref, k_ref, v_ref, dq_ref, dkdv_ref, m_ref, l_ref, dq_acc,
):
    width = head_count * HD
    for h in range(head_count):
        cols = slice(h * HD, (h + 1) * HD)
        m_ref[h] = jnp.full((BLK, 1), NEG_FILL, jnp.float32)
        l_ref[h] = jnp.zeros((BLK, 1), jnp.float32)
        dq_acc[:, cols] = jnp.zeros((BLK, HD), jnp.float32)

    def stat_body(j, carry):
        rows = pl.ds(pl.multiple_of(j * BLK, BLK), BLK)

        @pl.when(row_map[j] > 0)
        def _():
            for h in range(head_count):
                cols = slice(h * HD, (h + 1) * HD)
                scores = _nt(q_ref[:, cols], k_ref[rows, cols]) * score_scale
                old_max = m_ref[h]
                new_max = jnp.maximum(old_max, jnp.max(scores, axis=1, keepdims=True))
                kept = jnp.sum(jnp.exp(scores - new_max), axis=1, keepdims=True)
                l_ref[h] = l_ref[h] * jnp.exp(old_max - new_max) + kept
                m_ref[h] = new_max

        return carry

    lax.fori_loop(0, block_count, stat_body, 0)

    def back_body(j, carry):
        rows = pl.ds(pl.multiple_of(j * BLK, BLK), BLK)

        @pl.when(row_map[j] > 0)
        def _():
            for h in range(head_count):
                cols = slice(h * HD, (h + 1) * HD)
                q_h = q_ref[:, cols]
                do_h = do_ref[:, cols]
                k_b = k_ref[rows, cols]
                log_total = m_ref[h] + jnp.log(l_ref[h])
                row_delta = jnp.sum(
                    do_h.astype(jnp.float32) * o_ref[:, cols].astype(jnp.float32),
                    axis=1,
                    keepdims=True,
                )
                scores = _nt(q_h, k_b) * score_scale
                probs = jnp.exp(scores - log_total)
                dprobs = _nt(do_h, v_ref[rows, cols])
                score_gradient = (probs * (dprobs - row_delta) * score_scale).astype(jnp.bfloat16)
                dv = _tn(probs.astype(jnp.bfloat16), do_h)
                dk = _tn(score_gradient, q_h)
                dkdv_ref[rows, cols] = dk.astype(jnp.bfloat16)
                dkdv_ref[rows, pl.ds(width + h * HD, HD)] = dv.astype(jnp.bfloat16)
                part = jnp.dot(score_gradient, k_b, preferred_element_type=jnp.float32)
                dq_acc[:, cols] += part.astype(jnp.bfloat16).astype(jnp.float32)

        @pl.when(row_map[j] == 0)
        def _():
            dkdv_ref[rows, :] = jnp.zeros((BLK, 2 * width), jnp.bfloat16)

        return carry

    lax.fori_loop(0, block_count, back_body, 0)
    dq_ref[...] = dq_acc[...]


def slab_attention(row_map, queries, output_grad, attn_output, full_keys, full_values):
    slab_rows, width = queries.shape
    head_count = width // HD
    key_rows = full_keys.shape[0]
    block_count = key_rows // BLK
    vmem = pl.BlockSpec(memory_space=pltpu.VMEM)
    flops = 2 * slab_rows * key_rows * width * 6
    return pl.pallas_call(
        functools.partial(attention_kernel, head_count, block_count, 1.0 / math.sqrt(HD)),
        out_shape=(
            jax.ShapeDtypeStruct((slab_rows, width), jnp.float32),
            jax.ShapeDtypeStruct((key_rows, 2 * width), jnp.bfloat16),
        ),
        in_specs=[pl.BlockSpec(memory_space=pltpu.SMEM)] + [vmem] * 5,
        out_specs=(vmem, vmem),
        scratch_shapes=[
            pltpu.VMEM((head_count, slab_rows, 1), jnp.float32),
            pltpu.VMEM((head_count, slab_rows, 1), jnp.float32),
            pltpu.VMEM((slab_rows, width), jnp.float32),
        ],
        compiler_params=pltpu.CompilerParams(vmem_limit_bytes=48 * 1024 * 1024),
        cost_estimate=pl.CostEstimate(
            flops=flops,
            transcendentals=2 * slab_rows * key_rows * head_count,
            bytes_accessed=key_rows * width * 2 * 4,
        ),
    )(row_map, queries, output_grad, attn_output, full_keys, full_values)


def per_device(
    queries, key_states, value_states, attn_output, output_grad, block_map, w_query, w_key, w_value
):
    slab_rows, width = queries.shape
    context_count = lax.axis_size("ctx")
    row_map = lax.dynamic_index_in_dim(
        block_map, lax.axis_index("ctx") * slab_rows // BLK, axis=0, keepdims=False
    )
    key_value = jnp.concatenate([key_states, value_states], axis=1)
    spread = jnp.broadcast_to(key_value[None], (context_count,) + key_value.shape)
    gathered = lax.all_to_all(spread, "ctx", 0, 0, tiled=True).reshape(
        context_count * slab_rows, 2 * width
    )
    full_keys, full_values = gathered[:, :width], gathered[:, width:]
    dq_total, part_grads = slab_attention(
        row_map, queries, output_grad, attn_output, full_keys, full_values
    )
    local_grads = dq_total.astype(jnp.bfloat16)
    part_width = part_grads.shape[1]
    arrived = lax.all_to_all(
        part_grads.reshape(context_count, slab_rows, part_width),
        "ctx",
        split_axis=0,
        concat_axis=0,
        tiled=True,
    )
    finished = jnp.sum(arrived.astype(jnp.float32), axis=0).astype(jnp.bfloat16)
    own_grads = jnp.concatenate([local_grads, finished], axis=1)
    gradients = lax.all_gather(own_grads, "ctx", axis=0, tiled=True)
    projections = jnp.concatenate([w_query, w_key, w_value], axis=1)
    return lax.psum_scatter(
        lax.dot_general(
            gradients, projections, (((1,), (1,)), ((), ())), preferred_element_type=jnp.float32
        ).astype(jnp.bfloat16),
        "tp",
        scatter_dimension=0,
        tiled=True,
    )


def solution(mesh):
    return jax.shard_map(
        per_device,
        mesh=mesh,
        in_specs=(
            P("ctx", "tp"),
            P("ctx", "tp"),
            P("ctx", "tp"),
            P("ctx", "tp"),
            P("ctx", "tp"),
            P(),
            P("ctx", "tp"),
            P("ctx", "tp"),
            P("ctx", "tp"),
        ),
        out_specs=P("tp", "ctx"),
        check_vma=False,
    )
```

```python
import functools
import math

import jax
import jax.numpy as jnp
from jax import lax
from jax.experimental import pallas as pl
from jax.experimental.pallas import tpu as pltpu
from jax.sharding import PartitionSpec as P

HD = 128
BLK = 128


NEG_FILL = -1e30
GATHER_ORDER = (4, 2, 16, 8, 1)
SCATTER_ORDER = (1, 8, 16, 2, 4)
TP_ORDER = (1, 4, 8, 2)


def _nt(a, b):
    return lax.dot_general(a, b, (((1,), (1,)), ((), ())), preferred_element_type=jnp.float32)


def _tn(a, b):
    return lax.dot_general(a, b, (((0,), (0,)), ((), ())), preferred_element_type=jnp.float32)


def attention_kernel(
    head_count, block_count, score_scale,
    row_map, q_ref, do_ref, o_ref, k_ref, v_ref, dq_ref, dkdv_ref, m_ref, l_ref, dq_acc,
):
    width = head_count * HD
    for h in range(head_count):
        cols = slice(h * HD, (h + 1) * HD)
        m_ref[h] = jnp.full((BLK, 1), NEG_FILL, jnp.float32)
        l_ref[h] = jnp.zeros((BLK, 1), jnp.float32)
        dq_acc[:, cols] = jnp.zeros((BLK, HD), jnp.float32)

    def stat_body(j, carry):
        rows = pl.ds(pl.multiple_of(j * BLK, BLK), BLK)

        @pl.when(row_map[j] > 0)
        def _():
            for h in range(head_count):
                cols = slice(h * HD, (h + 1) * HD)
                scores = _nt(q_ref[:, cols], k_ref[rows, cols]) * score_scale
                old_max = m_ref[h]
                new_max = jnp.maximum(old_max, jnp.max(scores, axis=1, keepdims=True))
                kept = jnp.sum(jnp.exp(scores - new_max), axis=1, keepdims=True)
                l_ref[h] = l_ref[h] * jnp.exp(old_max - new_max) + kept
                m_ref[h] = new_max

        return carry

    lax.fori_loop(0, block_count, stat_body, 0)

    def back_body(j, carry):
        rows = pl.ds(pl.multiple_of(j * BLK, BLK), BLK)

        @pl.when(row_map[j] > 0)
        def _():
            for h in range(head_count):
                cols = slice(h * HD, (h + 1) * HD)
                q_h = q_ref[:, cols]
                do_h = do_ref[:, cols]
                k_b = k_ref[rows, cols]
                log_total = m_ref[h] + jnp.log(l_ref[h])
                row_delta = jnp.sum(
                    do_h.astype(jnp.float32) * o_ref[:, cols].astype(jnp.float32),
                    axis=1,
                    keepdims=True,
                )
                scores = _nt(q_h, k_b) * score_scale
                probs = jnp.exp(scores - log_total)
                dprobs = _nt(do_h, v_ref[rows, cols])
                score_gradient = (probs * (dprobs - row_delta) * score_scale).astype(jnp.bfloat16)
                dv = _tn(probs.astype(jnp.bfloat16), do_h)
                dk = _tn(score_gradient, q_h)
                dkdv_ref[rows, cols] = dk.astype(jnp.bfloat16)
                dkdv_ref[rows, pl.ds(width + h * HD, HD)] = dv.astype(jnp.bfloat16)
                part = jnp.dot(score_gradient, k_b, preferred_element_type=jnp.float32)
                dq_acc[:, cols] += part.astype(jnp.bfloat16).astype(jnp.float32)

        @pl.when(row_map[j] == 0)
        def _():
            dkdv_ref[rows, :] = jnp.zeros((BLK, 2 * width), jnp.bfloat16)

        return carry

    lax.fori_loop(0, block_count, back_body, 0)
    dq_ref[...] = dq_acc[...]


def slab_attention(row_map, queries, output_grad, attn_output, full_keys, full_values):
    slab_rows, width = queries.shape
    head_count = width // HD
    key_rows = full_keys.shape[0]
    block_count = key_rows // BLK
    vmem = pl.BlockSpec(memory_space=pltpu.VMEM)
    flops = 2 * slab_rows * key_rows * width * 6
    return pl.pallas_call(
        functools.partial(attention_kernel, head_count, block_count, 1.0 / math.sqrt(HD)),
        out_shape=(
            jax.ShapeDtypeStruct((slab_rows, width), jnp.float32),
            jax.ShapeDtypeStruct((key_rows, 2 * width), jnp.bfloat16),
        ),
        in_specs=[pl.BlockSpec(memory_space=pltpu.SMEM)] + [vmem] * 5,
        out_specs=(vmem, vmem),
        scratch_shapes=[
            pltpu.VMEM((head_count, slab_rows, 1), jnp.float32),
            pltpu.VMEM((head_count, slab_rows, 1), jnp.float32),
            pltpu.VMEM((slab_rows, width), jnp.float32),
        ],
        compiler_params=pltpu.CompilerParams(vmem_limit_bytes=48 * 1024 * 1024),
        cost_estimate=pl.CostEstimate(
            flops=flops,
            transcendentals=2 * slab_rows * key_rows * head_count,
            bytes_accessed=key_rows * width * 2 * 4,
        ),
    )(row_map, queries, output_grad, attn_output, full_keys, full_values)


def tree_gather(x, axis, order):
    me = lax.axis_index(axis)
    count = lax.axis_size(axis)
    held = x
    for distance in order:
        other = lax.ppermute(held, axis, [(i, i ^ distance) for i in range(count)])
        low = (me & distance) == 0
        held = jnp.where(low, jnp.stack([held, other]), jnp.stack([other, held]))
    bits = list(reversed(order))
    perm = sorted(range(len(bits)), key=lambda k: -bits[k])
    held = jnp.transpose(held, perm + list(range(len(bits), held.ndim)))
    return held.reshape((count * x.shape[0],) + x.shape[1:])


def tree_reduce_scatter(x, axis, order, wire=jnp.bfloat16):
    me = lax.axis_index(axis)
    count = lax.axis_size(axis)
    levels = count.bit_length() - 1
    block = x.shape[0] // count
    held = x.astype(jnp.float32).reshape((2,) * levels + (block,) + x.shape[1:])
    bits = [1 << (levels - 1 - k) for k in range(levels)]
    for distance in order:
        dim = bits.index(distance)
        bits.pop(dim)
        zero = lax.index_in_dim(held, 0, dim, keepdims=False)
        one = lax.index_in_dim(held, 1, dim, keepdims=False)
        low = (me & distance) == 0
        keep = jnp.where(low, zero, one)
        send = jnp.where(low, one, zero).astype(wire)
        other = lax.ppermute(send, axis, [(i, i ^ distance) for i in range(count)])
        held = keep + other.astype(jnp.float32)
    return held.reshape((block,) + x.shape[1:])


def per_device(
    queries, key_states, value_states, attn_output, output_grad, block_map, w_query, w_key, w_value
):
    slab_rows, width = queries.shape
    row_map = lax.dynamic_index_in_dim(
        block_map, lax.axis_index("ctx") * slab_rows // BLK, axis=0, keepdims=False
    )
    key_value = jnp.concatenate([key_states, value_states], axis=1)
    gathered = tree_gather(key_value, "ctx", GATHER_ORDER)
    full_keys, full_values = gathered[:, :width], gathered[:, width:]
    dq_total, part_grads = slab_attention(
        row_map, queries, output_grad, attn_output, full_keys, full_values
    )
    local_grads = dq_total.astype(jnp.bfloat16)
    finished = tree_reduce_scatter(part_grads, "ctx", SCATTER_ORDER).astype(jnp.bfloat16)
    own_grads = jnp.concatenate([local_grads, finished], axis=1)
    gradients = tree_gather(own_grads, "ctx", GATHER_ORDER)
    projections = jnp.concatenate([w_query, w_key, w_value], axis=1)
    term = lax.dot_general(
        gradients, projections, (((1,), (1,)), ((), ())), preferred_element_type=jnp.float32
    ).astype(jnp.bfloat16)
    return tree_reduce_scatter(term, "tp", TP_ORDER).astype(jnp.bfloat16)


def solution(mesh):
    return jax.shard_map(
        per_device,
        mesh=mesh,
        in_specs=(
            P("ctx", "tp"),
            P("ctx", "tp"),
            P("ctx", "tp"),
            P("ctx", "tp"),
            P("ctx", "tp"),
            P(),
            P("ctx", "tp"),
            P("ctx", "tp"),
            P("ctx", "tp"),
        ),
        out_specs=P("tp", "ctx"),
        check_vma=False,
    )
```

```python
import functools
import math

import jax
import jax.numpy as jnp
from jax import lax
from jax.experimental import pallas as pl
from jax.experimental.pallas import tpu as pltpu
from jax.sharding import PartitionSpec as P

HD = 128
BLK = 128


NEG_FILL = -1e30
GATHER_ORDERS = ((4, 2, 16, 8, 1), (4, 2, 16, 1, 8))
SCATTER_ORDERS = ((1, 8, 16, 2, 4), (8, 1, 16, 2, 4))
TP_ORDER = (1, 4, 8, 2)


def _nt(a, b):
    return lax.dot_general(a, b, (((1,), (1,)), ((), ())), preferred_element_type=jnp.float32)


def _tn(a, b):
    return lax.dot_general(a, b, (((0,), (0,)), ((), ())), preferred_element_type=jnp.float32)


def attention_kernel(
    head_count, block_count, score_scale,
    row_map, q_ref, do_ref, o_ref, k_ref, v_ref, dq_ref, dkdv_ref, m_ref, l_ref, dq_acc,
):
    width = head_count * HD
    for h in range(head_count):
        cols = slice(h * HD, (h + 1) * HD)
        m_ref[h] = jnp.full((BLK, 1), NEG_FILL, jnp.float32)
        l_ref[h] = jnp.zeros((BLK, 1), jnp.float32)
        dq_acc[:, cols] = jnp.zeros((BLK, HD), jnp.float32)

    def stat_body(j, carry):
        rows = pl.ds(pl.multiple_of(j * BLK, BLK), BLK)

        @pl.when(row_map[j] > 0)
        def _():
            for h in range(head_count):
                cols = slice(h * HD, (h + 1) * HD)
                scores = _nt(q_ref[:, cols], k_ref[rows, cols]) * score_scale
                old_max = m_ref[h]
                new_max = jnp.maximum(old_max, jnp.max(scores, axis=1, keepdims=True))
                kept = jnp.sum(jnp.exp(scores - new_max), axis=1, keepdims=True)
                l_ref[h] = l_ref[h] * jnp.exp(old_max - new_max) + kept
                m_ref[h] = new_max

        return carry

    lax.fori_loop(0, block_count, stat_body, 0)

    def back_body(j, carry):
        rows = pl.ds(pl.multiple_of(j * BLK, BLK), BLK)

        @pl.when(row_map[j] > 0)
        def _():
            for h in range(head_count):
                cols = slice(h * HD, (h + 1) * HD)
                q_h = q_ref[:, cols]
                do_h = do_ref[:, cols]
                k_b = k_ref[rows, cols]
                log_total = m_ref[h] + jnp.log(l_ref[h])
                row_delta = jnp.sum(
                    do_h.astype(jnp.float32) * o_ref[:, cols].astype(jnp.float32),
                    axis=1,
                    keepdims=True,
                )
                scores = _nt(q_h, k_b) * score_scale
                probs = jnp.exp(scores - log_total)
                dprobs = _nt(do_h, v_ref[rows, cols])
                score_gradient = (probs * (dprobs - row_delta) * score_scale).astype(jnp.bfloat16)
                dv = _tn(probs.astype(jnp.bfloat16), do_h)
                dk = _tn(score_gradient, q_h)
                dkdv_ref[rows, cols] = dk.astype(jnp.bfloat16)
                dkdv_ref[rows, pl.ds(width + h * HD, HD)] = dv.astype(jnp.bfloat16)
                part = jnp.dot(score_gradient, k_b, preferred_element_type=jnp.float32)
                dq_acc[:, cols] += part.astype(jnp.bfloat16).astype(jnp.float32)

        @pl.when(row_map[j] == 0)
        def _():
            dkdv_ref[rows, :] = jnp.zeros((BLK, 2 * width), jnp.bfloat16)

        return carry

    lax.fori_loop(0, block_count, back_body, 0)
    dq_ref[...] = dq_acc[...]


def slab_attention(row_map, queries, output_grad, attn_output, full_keys, full_values):
    slab_rows, width = queries.shape
    head_count = width // HD
    key_rows = full_keys.shape[0]
    block_count = key_rows // BLK
    vmem = pl.BlockSpec(memory_space=pltpu.VMEM)
    flops = 2 * slab_rows * key_rows * width * 6
    return pl.pallas_call(
        functools.partial(attention_kernel, head_count, block_count, 1.0 / math.sqrt(HD)),
        out_shape=(
            jax.ShapeDtypeStruct((slab_rows, width), jnp.float32),
            jax.ShapeDtypeStruct((key_rows, 2 * width), jnp.bfloat16),
        ),
        in_specs=[pl.BlockSpec(memory_space=pltpu.SMEM)] + [vmem] * 5,
        out_specs=(vmem, vmem),
        scratch_shapes=[
            pltpu.VMEM((head_count, slab_rows, 1), jnp.float32),
            pltpu.VMEM((head_count, slab_rows, 1), jnp.float32),
            pltpu.VMEM((slab_rows, width), jnp.float32),
        ],
        compiler_params=pltpu.CompilerParams(vmem_limit_bytes=48 * 1024 * 1024),
        cost_estimate=pl.CostEstimate(
            flops=flops,
            transcendentals=2 * slab_rows * key_rows * head_count,
            bytes_accessed=key_rows * width * 2 * 4,
        ),
    )(row_map, queries, output_grad, attn_output, full_keys, full_values)


def _pair_permute(value, distances):
    ctx_count, tp_count = lax.axis_size("ctx"), lax.axis_size("tp")
    pairs = [
        (c * tp_count + t, (c ^ distances[t % 2]) * tp_count + t)
        for c in range(ctx_count)
        for t in range(tp_count)
    ]
    return lax.ppermute(value, ("ctx", "tp"), pairs)


def core_tree_gather(x, orders):
    me = lax.axis_index("ctx")
    core = lax.axis_index("tp") % 2
    count = lax.axis_size("ctx")
    held = x
    for distances in zip(*orders):
        other = _pair_permute(held, distances)
        mine = jnp.where(core == 0, distances[0], distances[1])
        low = (me & mine) == 0
        held = jnp.where(low, jnp.stack([held, other]), jnp.stack([other, held]))
    results = []
    for order in orders:
        bits = list(reversed(order))
        perm = sorted(range(len(bits)), key=lambda k: -bits[k])
        results.append(
            jnp.transpose(held, perm + list(range(len(bits), held.ndim))).reshape(
                (count * x.shape[0],) + x.shape[1:]
            )
        )
    if tuple(orders[0]) == tuple(orders[1]):
        return results[0]
    return jnp.where(core == 0, results[0], results[1])


def core_tree_reduce_scatter(x, orders, wire=jnp.bfloat16):
    me = lax.axis_index("ctx")
    core = lax.axis_index("tp") % 2
    count = lax.axis_size("ctx")
    levels = count.bit_length() - 1
    block = x.shape[0] // count
    held = x.astype(jnp.float32).reshape((2,) * levels + (block,) + x.shape[1:])
    bits = [[1 << (levels - 1 - k) for k in range(levels)] for _ in orders]
    for distances in zip(*orders):
        keeps, sends = [], []
        for k, distance in enumerate(distances):
            dim = bits[k].index(distance)
            bits[k].pop(dim)
            zero = lax.index_in_dim(held, 0, dim, keepdims=False)
            one = lax.index_in_dim(held, 1, dim, keepdims=False)
            low = (me & distance) == 0
            keeps.append(jnp.where(low, zero, one))
            sends.append(jnp.where(low, one, zero))
        keep = jnp.where(core == 0, keeps[0], keeps[1])
        send = jnp.where(core == 0, sends[0], sends[1]).astype(wire)
        held = keep + _pair_permute(send, distances).astype(jnp.float32)
    return held.reshape((block,) + x.shape[1:])


def tree_reduce_scatter(x, axis, order, wire=jnp.bfloat16):
    me = lax.axis_index(axis)
    count = lax.axis_size(axis)
    levels = count.bit_length() - 1
    block = x.shape[0] // count
    held = x.astype(jnp.float32).reshape((2,) * levels + (block,) + x.shape[1:])
    bits = [1 << (levels - 1 - k) for k in range(levels)]
    for distance in order:
        dim = bits.index(distance)
        bits.pop(dim)
        zero = lax.index_in_dim(held, 0, dim, keepdims=False)
        one = lax.index_in_dim(held, 1, dim, keepdims=False)
        low = (me & distance) == 0
        keep = jnp.where(low, zero, one)
        send = jnp.where(low, one, zero).astype(wire)
        other = lax.ppermute(send, axis, [(i, i ^ distance) for i in range(count)])
        held = keep + other.astype(jnp.float32)
    return held.reshape((block,) + x.shape[1:])


def per_device(
    queries, key_states, value_states, attn_output, output_grad, block_map, w_query, w_key, w_value
):
    slab_rows, width = queries.shape
    row_map = lax.dynamic_index_in_dim(
        block_map, lax.axis_index("ctx") * slab_rows // BLK, axis=0, keepdims=False
    )
    key_value = jnp.concatenate([key_states, value_states], axis=1)
    gathered = core_tree_gather(key_value, GATHER_ORDERS)
    full_keys, full_values = gathered[:, :width], gathered[:, width:]
    dq_total, part_grads = slab_attention(
        row_map, queries, output_grad, attn_output, full_keys, full_values
    )
    local_grads = dq_total.astype(jnp.bfloat16)
    finished = core_tree_reduce_scatter(part_grads, SCATTER_ORDERS).astype(jnp.bfloat16)
    own_grads = jnp.concatenate([local_grads, finished], axis=1)
    gradients = core_tree_gather(own_grads, GATHER_ORDERS)
    projections = jnp.concatenate([w_query, w_key, w_value], axis=1)
    term = lax.dot_general(
        gradients, projections, (((1,), (1,)), ((), ())), preferred_element_type=jnp.float32
    ).astype(jnp.bfloat16)
    return tree_reduce_scatter(term, "tp", TP_ORDER).astype(jnp.bfloat16)


def solution(mesh):
    return jax.shard_map(
        per_device,
        mesh=mesh,
        in_specs=(
            P("ctx", "tp"),
            P("ctx", "tp"),
            P("ctx", "tp"),
            P("ctx", "tp"),
            P("ctx", "tp"),
            P(),
            P("ctx", "tp"),
            P("ctx", "tp"),
            P("ctx", "tp"),
        ),
        out_specs=P("tp", "ctx"),
        check_vma=False,
    )
```

```python
import functools
import math

import jax
import jax.numpy as jnp
from jax import lax
from jax.experimental import pallas as pl
from jax.experimental.pallas import tpu as pltpu
from jax.sharding import PartitionSpec as P

HD = 128
BLK = 128


NEG_FILL = -1e30
GATHER_ORDERS = ((4, 2, 16, 8, 1), (4, 2, 16, 1, 8))
SCATTER_ORDERS = ((1, 8, 16, 2, 4), (8, 1, 16, 2, 4))
TP_ORDER = (1, 4, 8, 2)


def _nt(a, b):
    return lax.dot_general(a, b, (((1,), (1,)), ((), ())), preferred_element_type=jnp.float32)


def _tn(a, b):
    return lax.dot_general(a, b, (((0,), (0,)), ((), ())), preferred_element_type=jnp.float32)


def attention_kernel(
    head_count, block_count, score_scale,
    tables, q_ref, do_ref, o_ref, kv_ref, dq_ref, dkdv_ref, m_ref, l_ref, dq_acc,
):
    width = head_count * HD
    for h in range(head_count):
        cols = slice(h * HD, (h + 1) * HD)
        m_ref[h] = jnp.full((BLK, 1), NEG_FILL, jnp.float32)
        l_ref[h] = jnp.zeros((BLK, 1), jnp.float32)
        dq_acc[:, cols] = jnp.zeros((BLK, HD), jnp.float32)

    def stat_body(j, carry):
        rows = pl.ds(pl.multiple_of(tables[1, j] * BLK, BLK), BLK)

        @pl.when(tables[0, j] > 0)
        def _():
            for h in range(head_count):
                cols = slice(h * HD, (h + 1) * HD)
                scores = _nt(q_ref[:, cols], kv_ref[rows, cols]) * score_scale
                old_max = m_ref[h]
                new_max = jnp.maximum(old_max, jnp.max(scores, axis=1, keepdims=True))
                kept = jnp.sum(jnp.exp(scores - new_max), axis=1, keepdims=True)
                l_ref[h] = l_ref[h] * jnp.exp(old_max - new_max) + kept
                m_ref[h] = new_max

        return carry

    lax.fori_loop(0, block_count, stat_body, 0)

    def back_body(j, carry):
        rows = pl.ds(pl.multiple_of(tables[1, j] * BLK, BLK), BLK)
        out_rows = pl.ds(pl.multiple_of(tables[2, j] * BLK, BLK), BLK)

        @pl.when(tables[0, j] > 0)
        def _():
            for h in range(head_count):
                cols = slice(h * HD, (h + 1) * HD)
                q_h = q_ref[:, cols]
                do_h = do_ref[:, cols]
                k_b = kv_ref[rows, cols]
                log_total = m_ref[h] + jnp.log(l_ref[h])
                row_delta = jnp.sum(
                    do_h.astype(jnp.float32) * o_ref[:, cols].astype(jnp.float32),
                    axis=1,
                    keepdims=True,
                )
                scores = _nt(q_h, k_b) * score_scale
                probs = jnp.exp(scores - log_total)
                dprobs = _nt(do_h, kv_ref[rows, pl.ds(width + h * HD, HD)])
                score_gradient = (probs * (dprobs - row_delta) * score_scale).astype(jnp.bfloat16)
                dv = _tn(probs.astype(jnp.bfloat16), do_h)
                dk = _tn(score_gradient, q_h)
                dkdv_ref[out_rows, cols] = dk.astype(jnp.bfloat16)
                dkdv_ref[out_rows, pl.ds(width + h * HD, HD)] = dv.astype(jnp.bfloat16)
                part = jnp.dot(score_gradient, k_b, preferred_element_type=jnp.float32)
                dq_acc[:, cols] += part.astype(jnp.bfloat16).astype(jnp.float32)

        @pl.when(tables[0, j] == 0)
        def _():
            dkdv_ref[out_rows, :] = jnp.zeros((BLK, 2 * width), jnp.bfloat16)

        return carry

    lax.fori_loop(0, block_count, back_body, 0)
    dq_ref[...] = dq_acc[...]


def slab_attention(tables, queries, output_grad, attn_output, key_value):
    slab_rows, width = queries.shape
    head_count = width // HD
    key_rows = key_value.shape[0]
    block_count = key_rows // BLK
    vmem = pl.BlockSpec(memory_space=pltpu.VMEM)
    flops = 2 * slab_rows * key_rows * width * 6
    return pl.pallas_call(
        functools.partial(attention_kernel, head_count, block_count, 1.0 / math.sqrt(HD)),
        out_shape=(
            jax.ShapeDtypeStruct((slab_rows, width), jnp.float32),
            jax.ShapeDtypeStruct((key_rows, 2 * width), jnp.bfloat16),
        ),
        in_specs=[pl.BlockSpec(memory_space=pltpu.SMEM)] + [vmem] * 4,
        out_specs=(vmem, vmem),
        scratch_shapes=[
            pltpu.VMEM((head_count, slab_rows, 1), jnp.float32),
            pltpu.VMEM((head_count, slab_rows, 1), jnp.float32),
            pltpu.VMEM((slab_rows, width), jnp.float32),
        ],
        compiler_params=pltpu.CompilerParams(vmem_limit_bytes=48 * 1024 * 1024),
        cost_estimate=pl.CostEstimate(
            flops=flops,
            transcendentals=2 * slab_rows * key_rows * head_count,
            bytes_accessed=key_rows * width * 2 * 4,
        ),
    )(tables, queries, output_grad, attn_output, key_value)


def _pair_permute(value, distances):
    ctx_count, tp_count = lax.axis_size("ctx"), lax.axis_size("tp")
    pairs = [
        (c * tp_count + t, (c ^ distances[t % 2]) * tp_count + t)
        for c in range(ctx_count)
        for t in range(tp_count)
    ]
    return lax.ppermute(value, ("ctx", "tp"), pairs)


def gather_positions(me, distances, count):
    offset = me ^ jnp.arange(count, dtype=jnp.int32)
    return sum(((offset & d) != 0).astype(jnp.int32) << r for r, d in enumerate(distances))


def scatter_positions(me, distances, count):
    offset = me ^ jnp.arange(count, dtype=jnp.int32)
    top = len(distances) - 1
    return sum(((offset & d) == 0).astype(jnp.int32) << (top - r) for r, d in enumerate(distances))


def per_core(core, tables):
    return jnp.where(core == 0, tables[0], tables[1])


def concat_gather(x, orders):
    held = x
    for distances in zip(*orders):
        held = jnp.concatenate([held, _pair_permute(held, distances)], axis=0)
    return held


def halving_reduce(x, orders, wire=jnp.bfloat16):
    held = x
    for distances in zip(*orders):
        half = held.shape[0] // 2
        sent = _pair_permute(held[:half].astype(wire), distances)
        held = held[half:].astype(jnp.float32) + sent.astype(jnp.float32)
    return held


def tp_halving_reduce(x, order, wire=jnp.bfloat16):
    count = lax.axis_size("tp")
    held = x
    for distance in order:
        half = held.shape[0] // 2
        sent = lax.ppermute(
            held[:half].astype(wire), "tp", [(i, i ^ distance) for i in range(count)]
        )
        held = held[half:].astype(jnp.float32) + sent.astype(jnp.float32)
    return held


def per_device(
    queries, key_states, value_states, attn_output, output_grad, block_map, w_query, w_key, w_value
):
    slab_rows, width = queries.shape
    ctx_count, tp_count = lax.axis_size("ctx"), lax.axis_size("tp")
    me = lax.axis_index("ctx")
    me_tp = lax.axis_index("tp")
    core = me_tp % 2
    row_map = lax.dynamic_index_in_dim(block_map, me * slab_rows // BLK, axis=0, keepdims=False)
    gather_at = per_core(core, [gather_positions(me, o, ctx_count) for o in GATHER_ORDERS])
    scatter_at = per_core(core, [scatter_positions(me, o, ctx_count) for o in SCATTER_ORDERS])
    tables = jnp.stack([row_map.astype(jnp.int32), gather_at, scatter_at])
    key_value = jnp.concatenate([key_states, value_states], axis=1)
    gathered = concat_gather(key_value, GATHER_ORDERS)
    dq_total, part_grads = slab_attention(tables, queries, output_grad, attn_output, gathered)
    finished = halving_reduce(part_grads, SCATTER_ORDERS).astype(jnp.bfloat16)
    own_grads = jnp.concatenate([dq_total.astype(jnp.bfloat16), finished], axis=1)
    gradients = concat_gather(own_grads, GATHER_ORDERS)
    projections = jnp.concatenate([w_query, w_key, w_value], axis=1)
    term = lax.dot_general(
        gradients, projections, (((1,), (1,)), ((), ())), preferred_element_type=jnp.float32
    ).astype(jnp.bfloat16)
    tp_at = scatter_positions(me_tp, TP_ORDER, tp_count)
    owner = jnp.argsort(tp_at)
    per_owner = ctx_count // tp_count
    wanted = (owner[:, None] * per_owner + jnp.arange(per_owner)[None, :]).reshape(-1)
    source = gather_at[wanted]
    ordered = jnp.take(term.reshape(ctx_count, slab_rows, -1), source, axis=0)
    return tp_halving_reduce(ordered.reshape(ctx_count * slab_rows, -1), TP_ORDER).astype(
        jnp.bfloat16
    )


def solution(mesh):
    return jax.shard_map(
        per_device,
        mesh=mesh,
        in_specs=(
            P("ctx", "tp"),
            P("ctx", "tp"),
            P("ctx", "tp"),
            P("ctx", "tp"),
            P("ctx", "tp"),
            P(),
            P("ctx", "tp"),
            P("ctx", "tp"),
            P("ctx", "tp"),
        ),
        out_specs=P("tp", "ctx"),
        check_vma=False,
    )
```

```python
import functools
import math

import jax
import jax.numpy as jnp
from jax import lax
from jax.experimental import pallas as pl
from jax.experimental.pallas import tpu as pltpu
from jax.sharding import PartitionSpec as P

HD = 128
BLK = 128


NEG_FILL = -1e30
GATHER_ORDERS = ((4, 2, 16, 8, 1), (4, 2, 16, 1, 8))
SCATTER_ORDERS = ((1, 8, 16, 2, 4), (8, 1, 16, 2, 4))
TP_ORDER = (1, 4, 8, 2)


def _nt(a, b):
    return lax.dot_general(a, b, (((1,), (1,)), ((), ())), preferred_element_type=jnp.float32)


def _tn(a, b):
    return lax.dot_general(a, b, (((0,), (0,)), ((), ())), preferred_element_type=jnp.float32)


def attention_kernel(head_count, score_scale, mask_ref, q_ref, do_ref, o_ref, kv_ref, dq_ref, dkdv_ref):
    width = head_count * HD
    key_rows = kv_ref.shape[0]
    block_count = key_rows // BLK
    allowed = mask_ref[0:1, :] > 0
    for h in range(head_count):
        cols = slice(h * HD, (h + 1) * HD)
        q_h = q_ref[:, cols]
        do_h = do_ref[:, cols]
        k_h = kv_ref[:, cols]
        scores = _nt(q_h, k_h) * score_scale
        masked = jnp.where(allowed, scores, NEG_FILL)
        row_max = jnp.max(masked, axis=1, keepdims=True)
        row_sum = jnp.sum(jnp.where(allowed, jnp.exp(masked - row_max), 0.0), axis=1, keepdims=True)
        log_total = row_max + jnp.log(row_sum)
        probs = jnp.where(allowed, jnp.exp(masked - log_total), 0.0)
        row_delta = jnp.sum(
            do_h.astype(jnp.float32) * o_ref[:, cols].astype(jnp.float32), axis=1, keepdims=True
        )
        dprobs = _nt(do_h, kv_ref[:, pl.ds(width + h * HD, HD)])
        score_gradient = (probs * (dprobs - row_delta) * score_scale).astype(jnp.bfloat16)
        dq_ref[:, cols] = jnp.dot(score_gradient, k_h, preferred_element_type=jnp.float32)
        dk = _tn(score_gradient, q_h).astype(jnp.bfloat16)
        dv = _tn(probs.astype(jnp.bfloat16), do_h).astype(jnp.bfloat16)
        for p in range(block_count):
            src = slice(p * BLK, (p + 1) * BLK)
            dst = slice((block_count - 1 - p) * BLK, (block_count - p) * BLK)
            dkdv_ref[dst, cols] = dk[src]
            dkdv_ref[dst, pl.ds(width + h * HD, HD)] = dv[src]


def slab_attention(mask, queries, output_grad, attn_output, key_value):
    slab_rows, width = queries.shape
    head_count = width // HD
    key_rows = key_value.shape[0]
    vmem = pl.BlockSpec(memory_space=pltpu.VMEM)
    flops = 2 * slab_rows * key_rows * width * 5
    return pl.pallas_call(
        functools.partial(attention_kernel, head_count, 1.0 / math.sqrt(HD)),
        out_shape=(
            jax.ShapeDtypeStruct((slab_rows, width), jnp.float32),
            jax.ShapeDtypeStruct((key_rows, 2 * width), jnp.bfloat16),
        ),
        in_specs=[vmem] * 5,
        out_specs=(vmem, vmem),
        compiler_params=pltpu.CompilerParams(vmem_limit_bytes=48 * 1024 * 1024),
        cost_estimate=pl.CostEstimate(
            flops=flops,
            transcendentals=2 * slab_rows * key_rows * head_count,
            bytes_accessed=key_rows * width * 2 * 4,
        ),
    )(mask, queries, output_grad, attn_output, key_value)


def _pair_permute(value, distances):
    ctx_count, tp_count = lax.axis_size("ctx"), lax.axis_size("tp")
    pairs = [
        (c * tp_count + t, (c ^ distances[t % 2]) * tp_count + t)
        for c in range(ctx_count)
        for t in range(tp_count)
    ]
    return lax.ppermute(value, ("ctx", "tp"), pairs)


def gather_positions(me, distances, count):
    offset = me ^ jnp.arange(count, dtype=jnp.int32)
    return sum(((offset & d) != 0).astype(jnp.int32) << r for r, d in enumerate(distances))


def scatter_positions(me, distances, count):
    offset = me ^ jnp.arange(count, dtype=jnp.int32)
    top = len(distances) - 1
    return sum(((offset & d) == 0).astype(jnp.int32) << (top - r) for r, d in enumerate(distances))


def per_core(core, tables):
    return jnp.where(core == 0, tables[0], tables[1])


def concat_gather(x, orders):
    held = x
    for distances in zip(*orders):
        held = jnp.concatenate([held, _pair_permute(held, distances)], axis=0)
    return held


def halving_reduce(x, orders, wire=jnp.bfloat16):
    held = x
    for distances in zip(*orders):
        half = held.shape[0] // 2
        sent = _pair_permute(held[:half].astype(wire), distances)
        held = held[half:].astype(jnp.float32) + sent.astype(jnp.float32)
    return held


def tp_halving_reduce(x, order, wire=jnp.bfloat16):
    count = lax.axis_size("tp")
    held = x
    for distance in order:
        half = held.shape[0] // 2
        sent = lax.ppermute(
            held[:half].astype(wire), "tp", [(i, i ^ distance) for i in range(count)]
        )
        held = held[half:].astype(jnp.float32) + sent.astype(jnp.float32)
    return held


def per_device(
    queries, key_states, value_states, attn_output, output_grad, block_map, w_query, w_key, w_value
):
    slab_rows, width = queries.shape
    ctx_count, tp_count = lax.axis_size("ctx"), lax.axis_size("tp")
    me = lax.axis_index("ctx")
    me_tp = lax.axis_index("tp")
    core = me_tp % 2
    row_map = lax.dynamic_index_in_dim(block_map, me * slab_rows // BLK, axis=0, keepdims=False)
    gather_at = per_core(core, [gather_positions(me, o, ctx_count) for o in GATHER_ORDERS])
    slab_at = jnp.argsort(gather_at)
    mask = jnp.broadcast_to(
        jnp.repeat(row_map[slab_at].astype(jnp.float32), BLK)[None, :], (8, ctx_count * slab_rows)
    )
    key_value = jnp.concatenate([key_states, value_states], axis=1)
    gathered = concat_gather(key_value, GATHER_ORDERS)
    dq_total, part_grads = slab_attention(mask, queries, output_grad, attn_output, gathered)
    finished = halving_reduce(part_grads, SCATTER_ORDERS).astype(jnp.bfloat16)
    own_grads = jnp.concatenate([dq_total.astype(jnp.bfloat16), finished], axis=1)
    gradients = concat_gather(own_grads, GATHER_ORDERS)
    projections = jnp.concatenate([w_query, w_key, w_value], axis=1)
    term = lax.dot_general(
        gradients, projections, (((1,), (1,)), ((), ())), preferred_element_type=jnp.float32
    ).astype(jnp.bfloat16)
    tp_at = scatter_positions(me_tp, TP_ORDER, tp_count)
    owner = jnp.argsort(tp_at)
    per_owner = ctx_count // tp_count
    wanted = (owner[:, None] * per_owner + jnp.arange(per_owner)[None, :]).reshape(-1)
    source = gather_at[wanted]
    ordered = jnp.take(term.reshape(ctx_count, slab_rows, -1), source, axis=0)
    return tp_halving_reduce(ordered.reshape(ctx_count * slab_rows, -1), TP_ORDER).astype(
        jnp.bfloat16
    )


def solution(mesh):
    return jax.shard_map(
        per_device,
        mesh=mesh,
        in_specs=(
            P("ctx", "tp"),
            P("ctx", "tp"),
            P("ctx", "tp"),
            P("ctx", "tp"),
            P("ctx", "tp"),
            P(),
            P("ctx", "tp"),
            P("ctx", "tp"),
            P("ctx", "tp"),
        ),
        out_specs=P("tp", "ctx"),
        check_vma=False,
    )
```

```python
import functools
import math

import jax
import jax.numpy as jnp
from jax import lax
from jax.experimental import pallas as pl
from jax.experimental.pallas import tpu as pltpu
from jax.sharding import PartitionSpec as P

HD = 128
BLK = 128


NEG_FILL = -1e30
GATHER_ORDERS = ((4, 2, 16, 8, 1), (4, 2, 16, 1, 8))
SCATTER_ORDERS = ((1, 8, 16, 2, 4), (8, 1, 16, 2, 4))
TP_ORDER = (1, 4, 8, 2)


def _nt(a, b):
    return lax.dot_general(a, b, (((1,), (1,)), ((), ())), preferred_element_type=jnp.float32)


def _tn(a, b):
    return lax.dot_general(a, b, (((0,), (0,)), ((), ())), preferred_element_type=jnp.float32)


def attention_kernel(head_count, score_scale, mask_ref, q_ref, do_ref, o_ref, kv_ref, dq_ref, dkdv_ref):
    width = head_count * HD
    key_rows = kv_ref.shape[0]
    block_count = key_rows // BLK
    allowed = mask_ref[0:1, :] > 0
    for h in range(head_count):
        cols = slice(h * HD, (h + 1) * HD)
        q_h = q_ref[:, cols]
        do_h = do_ref[:, cols]
        k_h = kv_ref[:, cols]
        scores = _nt(q_h, k_h) * score_scale
        masked = jnp.where(allowed, scores, NEG_FILL)
        row_max = jnp.max(masked, axis=1, keepdims=True)
        row_sum = jnp.sum(jnp.where(allowed, jnp.exp(masked - row_max), 0.0), axis=1, keepdims=True)
        log_total = row_max + jnp.log(row_sum)
        probs = jnp.where(allowed, jnp.exp(masked - log_total), 0.0)
        row_delta = jnp.sum(
            do_h.astype(jnp.float32) * o_ref[:, cols].astype(jnp.float32), axis=1, keepdims=True
        )
        dprobs = _nt(do_h, kv_ref[:, pl.ds(width + h * HD, HD)])
        score_gradient = (probs * (dprobs - row_delta) * score_scale).astype(jnp.bfloat16)
        dq_ref[:, cols] = jnp.dot(score_gradient, k_h, preferred_element_type=jnp.float32)
        dk = _tn(score_gradient, q_h).astype(jnp.bfloat16)
        dv = _tn(probs.astype(jnp.bfloat16), do_h).astype(jnp.bfloat16)
        for p in range(block_count):
            src = slice(p * BLK, (p + 1) * BLK)
            dst = slice((block_count - 1 - p) * BLK, (block_count - p) * BLK)
            dkdv_ref[dst, cols] = dk[src]
            dkdv_ref[dst, pl.ds(width + h * HD, HD)] = dv[src]


def slab_attention(mask, queries, output_grad, attn_output, key_value):
    slab_rows, width = queries.shape
    head_count = width // HD
    key_rows = key_value.shape[0]
    vmem = pl.BlockSpec(memory_space=pltpu.VMEM)
    flops = 2 * slab_rows * key_rows * width * 5
    return pl.pallas_call(
        functools.partial(attention_kernel, head_count, 1.0 / math.sqrt(HD)),
        out_shape=(
            jax.ShapeDtypeStruct((slab_rows, width), jnp.float32),
            jax.ShapeDtypeStruct((key_rows, 2 * width), jnp.bfloat16),
        ),
        in_specs=[vmem] * 5,
        out_specs=(vmem, vmem),
        compiler_params=pltpu.CompilerParams(vmem_limit_bytes=48 * 1024 * 1024),
        cost_estimate=pl.CostEstimate(
            flops=flops,
            transcendentals=2 * slab_rows * key_rows * head_count,
            bytes_accessed=key_rows * width * 2 * 4,
        ),
    )(mask, queries, output_grad, attn_output, key_value)


def _pair_permute(value, distances):
    ctx_count, tp_count = lax.axis_size("ctx"), lax.axis_size("tp")
    pairs = [
        (c * tp_count + t, (c ^ distances[t % 2]) * tp_count + t)
        for c in range(ctx_count)
        for t in range(tp_count)
    ]
    return lax.ppermute(value, ("ctx", "tp"), pairs)


def gather_positions(me, distances, count):
    offset = me ^ jnp.arange(count, dtype=jnp.int32)
    return sum(((offset & d) != 0).astype(jnp.int32) << r for r, d in enumerate(distances))


def scatter_positions(me, distances, count):
    offset = me ^ jnp.arange(count, dtype=jnp.int32)
    top = len(distances) - 1
    return sum(((offset & d) == 0).astype(jnp.int32) << (top - r) for r, d in enumerate(distances))


def per_core(core, tables):
    return jnp.where(core == 0, tables[0], tables[1])


def concat_gather(x, orders):
    held = x
    for distances in zip(*orders):
        held = jnp.concatenate([held, _pair_permute(held, distances)], axis=0)
    return held


def halving_reduce(x, orders, wire=jnp.bfloat16):
    held = x
    for distances in zip(*orders):
        half = held.shape[0] // 2
        sent = _pair_permute(held[:half].astype(wire), distances)
        held = held[half:].astype(jnp.float32) + sent.astype(jnp.float32)
    return held


def tp_halving_reduce(x, order, wire=jnp.bfloat16):
    count = lax.axis_size("tp")
    held = x
    for distance in order:
        half = held.shape[0] // 2
        sent = lax.ppermute(
            held[:half].astype(wire), "tp", [(i, i ^ distance) for i in range(count)]
        )
        held = held[half:].astype(jnp.float32) + sent.astype(jnp.float32)
    return held


def per_device(
    queries, key_states, value_states, attn_output, output_grad, block_map, w_query, w_key, w_value
):
    slab_rows, width = queries.shape
    ctx_count, tp_count = lax.axis_size("ctx"), lax.axis_size("tp")
    me = lax.axis_index("ctx")
    me_tp = lax.axis_index("tp")
    core = me_tp % 2
    row_map = lax.dynamic_index_in_dim(block_map, me * slab_rows // BLK, axis=0, keepdims=False)
    gather_at = per_core(core, [gather_positions(me, o, ctx_count) for o in GATHER_ORDERS])
    slab_at = jnp.argsort(gather_at)
    mask = jnp.broadcast_to(
        jnp.repeat(row_map[slab_at].astype(jnp.float32), BLK)[None, :], (8, ctx_count * slab_rows)
    )
    key_value = jnp.concatenate([key_states, value_states], axis=1)
    gathered = concat_gather(key_value, GATHER_ORDERS)
    dq_total, part_grads = slab_attention(mask, queries, output_grad, attn_output, gathered)
    last = tuple(order[-1] for order in SCATTER_ORDERS)
    assert last == tuple(order[0] for order in GATHER_ORDERS)
    held = halving_reduce(part_grads, tuple(order[:-1] for order in SCATTER_ORDERS))
    theirs_part, mine_part = held[:slab_rows], held[slab_rows:]
    dq_low = dq_total.astype(jnp.bfloat16)
    payload = jnp.concatenate(
        [theirs_part.astype(jnp.bfloat16), mine_part.astype(jnp.bfloat16), dq_low], axis=1
    )
    arrived = _pair_permute(payload, last)
    part_width = mine_part.shape[1]
    mine = mine_part + arrived[:, :part_width].astype(jnp.float32)
    theirs = theirs_part + arrived[:, part_width : 2 * part_width].astype(jnp.float32)
    paired = jnp.concatenate(
        [
            jnp.concatenate([dq_low, mine.astype(jnp.bfloat16)], axis=1),
            jnp.concatenate([arrived[:, 2 * part_width :], theirs.astype(jnp.bfloat16)], axis=1),
        ],
        axis=0,
    )
    gradients = concat_gather(paired, tuple(order[1:] for order in GATHER_ORDERS))
    projections = jnp.concatenate([w_query, w_key, w_value], axis=1)
    term = lax.dot_general(
        gradients, projections, (((1,), (1,)), ((), ())), preferred_element_type=jnp.float32
    ).astype(jnp.bfloat16)
    tp_at = scatter_positions(me_tp, TP_ORDER, tp_count)
    owner = jnp.argsort(tp_at)
    per_owner = ctx_count // tp_count
    wanted = (owner[:, None] * per_owner + jnp.arange(per_owner)[None, :]).reshape(-1)
    source = gather_at[wanted]
    ordered = jnp.take(term.reshape(ctx_count, slab_rows, -1), source, axis=0)
    return tp_halving_reduce(ordered.reshape(ctx_count * slab_rows, -1), TP_ORDER).astype(
        jnp.bfloat16
    )


def solution(mesh):
    return jax.shard_map(
        per_device,
        mesh=mesh,
        in_specs=(
            P("ctx", "tp"),
            P("ctx", "tp"),
            P("ctx", "tp"),
            P("ctx", "tp"),
            P("ctx", "tp"),
            P(),
            P("ctx", "tp"),
            P("ctx", "tp"),
            P("ctx", "tp"),
        ),
        out_specs=P("tp", "ctx"),
        check_vma=False,
    )
```

```python
import functools
import math

import jax
import jax.numpy as jnp
from jax import lax
from jax.experimental import pallas as pl
from jax.experimental.pallas import tpu as pltpu
from jax.sharding import PartitionSpec as P

HD = 128
BLK = 128


NEG_FILL = -1e30
GATHER_ORDERS = ((4, 2, 16, 8, 1), (4, 16, 2, 1, 8))
SCATTER_ORDERS = tuple(tuple(reversed(order)) for order in GATHER_ORDERS)
TP_ORDER = (1, 4, 8, 2)


def _nt(a, b):
    return lax.dot_general(a, b, (((1,), (1,)), ((), ())), preferred_element_type=jnp.float32)


def _tn(a, b):
    return lax.dot_general(a, b, (((0,), (0,)), ((), ())), preferred_element_type=jnp.float32)


def attention_kernel(head_count, score_scale, mask_ref, q_ref, do_ref, o_ref, kv_ref, dq_ref, dkdv_ref):
    width = head_count * HD
    key_rows = kv_ref.shape[0]
    block_count = key_rows // BLK
    allowed = mask_ref[0:1, :] > 0
    for h in range(head_count):
        cols = slice(h * HD, (h + 1) * HD)
        q_h = q_ref[:, cols]
        do_h = do_ref[:, cols]
        k_h = kv_ref[:, cols]
        scores = _nt(q_h, k_h) * score_scale
        masked = jnp.where(allowed, scores, NEG_FILL)
        row_max = jnp.max(masked, axis=1, keepdims=True)
        row_sum = jnp.sum(jnp.where(allowed, jnp.exp(masked - row_max), 0.0), axis=1, keepdims=True)
        log_total = row_max + jnp.log(row_sum)
        probs = jnp.where(allowed, jnp.exp(masked - log_total), 0.0)
        row_delta = jnp.sum(
            do_h.astype(jnp.float32) * o_ref[:, cols].astype(jnp.float32), axis=1, keepdims=True
        )
        dprobs = _nt(do_h, kv_ref[:, pl.ds(width + h * HD, HD)])
        score_gradient = (probs * (dprobs - row_delta) * score_scale).astype(jnp.bfloat16)
        dq_ref[:, cols] = jnp.dot(score_gradient, k_h, preferred_element_type=jnp.float32)
        dk = _tn(score_gradient, q_h).astype(jnp.bfloat16)
        dv = _tn(probs.astype(jnp.bfloat16), do_h).astype(jnp.bfloat16)
        for p in range(block_count):
            src = slice(p * BLK, (p + 1) * BLK)
            dst = slice((block_count - 1 - p) * BLK, (block_count - p) * BLK)
            dkdv_ref[dst, cols] = dk[src]
            dkdv_ref[dst, pl.ds(width + h * HD, HD)] = dv[src]


def slab_attention(mask, queries, output_grad, attn_output, key_value):
    slab_rows, width = queries.shape
    head_count = width // HD
    key_rows = key_value.shape[0]
    vmem = pl.BlockSpec(memory_space=pltpu.VMEM)
    flops = 2 * slab_rows * key_rows * width * 5
    return pl.pallas_call(
        functools.partial(attention_kernel, head_count, 1.0 / math.sqrt(HD)),
        out_shape=(
            jax.ShapeDtypeStruct((slab_rows, width), jnp.float32),
            jax.ShapeDtypeStruct((key_rows, 2 * width), jnp.bfloat16),
        ),
        in_specs=[vmem] * 5,
        out_specs=(vmem, vmem),
        compiler_params=pltpu.CompilerParams(vmem_limit_bytes=48 * 1024 * 1024),
        cost_estimate=pl.CostEstimate(
            flops=flops,
            transcendentals=2 * slab_rows * key_rows * head_count,
            bytes_accessed=key_rows * width * 2 * 4,
        ),
    )(mask, queries, output_grad, attn_output, key_value)


def _pair_permute(value, distances):
    ctx_count, tp_count = lax.axis_size("ctx"), lax.axis_size("tp")
    pairs = [
        (c * tp_count + t, (c ^ distances[t % 2]) * tp_count + t)
        for c in range(ctx_count)
        for t in range(tp_count)
    ]
    return lax.ppermute(value, ("ctx", "tp"), pairs)


def gather_positions(me, distances, count):
    offset = me ^ jnp.arange(count, dtype=jnp.int32)
    return sum(((offset & d) != 0).astype(jnp.int32) << r for r, d in enumerate(distances))


def scatter_positions(me, distances, count):
    offset = me ^ jnp.arange(count, dtype=jnp.int32)
    top = len(distances) - 1
    return sum(((offset & d) == 0).astype(jnp.int32) << (top - r) for r, d in enumerate(distances))


def per_core(core, tables):
    return jnp.where(core == 0, tables[0], tables[1])


def concat_gather(x, orders):
    held = x
    for distances in zip(*orders):
        held = jnp.concatenate([held, _pair_permute(held, distances)], axis=0)
    return held


def halving_reduce(x, orders, wire=jnp.bfloat16):
    held = x
    for distances in zip(*orders):
        half = held.shape[0] // 2
        sent = _pair_permute(held[:half].astype(wire), distances)
        held = held[half:].astype(jnp.float32) + sent.astype(jnp.float32)
    return held


def tp_halving_reduce(x, order, wire=jnp.bfloat16):
    count = lax.axis_size("tp")
    held = x
    for distance in order:
        half = held.shape[0] // 2
        sent = lax.ppermute(
            held[:half].astype(wire), "tp", [(i, i ^ distance) for i in range(count)]
        )
        held = held[half:].astype(jnp.float32) + sent.astype(jnp.float32)
    return held


def per_device(
    queries, key_states, value_states, attn_output, output_grad, block_map, w_query, w_key, w_value
):
    slab_rows, width = queries.shape
    ctx_count, tp_count = lax.axis_size("ctx"), lax.axis_size("tp")
    me = lax.axis_index("ctx")
    me_tp = lax.axis_index("tp")
    core = me_tp % 2
    row_map = lax.dynamic_index_in_dim(block_map, me * slab_rows // BLK, axis=0, keepdims=False)
    gather_at = per_core(core, [gather_positions(me, o, ctx_count) for o in GATHER_ORDERS])
    slab_at = jnp.argsort(gather_at)
    mask = jnp.broadcast_to(
        jnp.repeat(row_map[slab_at].astype(jnp.float32), BLK)[None, :], (8, ctx_count * slab_rows)
    )
    key_value = jnp.concatenate([key_states, value_states], axis=1)
    gathered = concat_gather(key_value, GATHER_ORDERS)
    dq_total, part_grads = slab_attention(mask, queries, output_grad, attn_output, gathered)
    finished = halving_reduce(part_grads, SCATTER_ORDERS).astype(jnp.bfloat16)
    own_grads = jnp.concatenate([dq_total.astype(jnp.bfloat16), finished], axis=1)
    gradients = concat_gather(own_grads, GATHER_ORDERS)
    projections = jnp.concatenate([w_query, w_key, w_value], axis=1)
    term = lax.dot_general(
        gradients, projections, (((1,), (1,)), ((), ())), preferred_element_type=jnp.float32
    ).astype(jnp.bfloat16)
    tp_at = scatter_positions(me_tp, TP_ORDER, tp_count)
    owner = jnp.argsort(tp_at)
    per_owner = ctx_count // tp_count
    wanted = (owner[:, None] * per_owner + jnp.arange(per_owner)[None, :]).reshape(-1)
    source = gather_at[wanted]
    ordered = jnp.take(term.reshape(ctx_count, slab_rows, -1), source, axis=0)
    return tp_halving_reduce(ordered.reshape(ctx_count * slab_rows, -1), TP_ORDER).astype(
        jnp.bfloat16
    )


def solution(mesh):
    return jax.shard_map(
        per_device,
        mesh=mesh,
        in_specs=(
            P("ctx", "tp"),
            P("ctx", "tp"),
            P("ctx", "tp"),
            P("ctx", "tp"),
            P("ctx", "tp"),
            P(),
            P("ctx", "tp"),
            P("ctx", "tp"),
            P("ctx", "tp"),
        ),
        out_specs=P("tp", "ctx"),
        check_vma=False,
    )
```

```python
import functools
import math

import jax
import jax.numpy as jnp
from jax import lax
from jax.experimental import pallas as pl
from jax.experimental.pallas import tpu as pltpu
from jax.sharding import PartitionSpec as P

HD = 128
BLK = 128


NEG_FILL = -1e30
GATHER_ORDERS = ((4, 2, 16, 8, 1), (4, 16, 2, 1, 8))
SCATTER_ORDERS = tuple(tuple(reversed(order)) for order in GATHER_ORDERS)
HEAD_GATHER_ORDERS = ((4, 2, 16, 8), (4, 16, 2, 8))
HEAD_SCATTER_ORDERS = tuple(tuple(reversed(order)) for order in HEAD_GATHER_ORDERS)
TP_ORDER = (1, 4, 8, 2)


def _nt(a, b):
    return lax.dot_general(a, b, (((1,), (1,)), ((), ())), preferred_element_type=jnp.float32)


def _tn(a, b):
    return lax.dot_general(a, b, (((0,), (0,)), ((), ())), preferred_element_type=jnp.float32)


def attention_kernel(slab_count, score_scale, mask_ref, q_ref, do_ref, o_ref, kv_ref, dq_ref, dkdv_ref):
    key_rows = kv_ref.shape[0]
    rows = q_ref.shape[0] // slab_count
    block = rows * slab_count
    block_count = key_rows // block
    k_h = kv_ref[:, 0:HD]
    dk_total = jnp.zeros((key_rows, HD), jnp.float32)
    dv_total = jnp.zeros((key_rows, HD), jnp.float32)
    for a in range(slab_count):
        mine = slice(a * rows, (a + 1) * rows)
        allowed = mask_ref[a : a + 1, :] > 0
        q_h = q_ref[mine, :]
        do_h = do_ref[mine, :]
        scores = _nt(q_h, k_h) * score_scale
        masked = jnp.where(allowed, scores, NEG_FILL)
        row_max = jnp.max(masked, axis=1, keepdims=True)
        row_sum = jnp.sum(jnp.where(allowed, jnp.exp(masked - row_max), 0.0), axis=1, keepdims=True)
        log_total = row_max + jnp.log(row_sum)
        probs = jnp.where(allowed, jnp.exp(masked - log_total), 0.0)
        row_delta = jnp.sum(
            do_h.astype(jnp.float32) * o_ref[mine, :].astype(jnp.float32), axis=1, keepdims=True
        )
        dprobs = _nt(do_h, kv_ref[:, HD : 2 * HD])
        score_gradient = (probs * (dprobs - row_delta) * score_scale).astype(jnp.bfloat16)
        dq_ref[mine, :] = jnp.dot(score_gradient, k_h, preferred_element_type=jnp.float32)
        dk_total = dk_total + _tn(score_gradient, q_h)
        dv_total = dv_total + _tn(probs.astype(jnp.bfloat16), do_h)
    dk = dk_total.astype(jnp.bfloat16)
    dv = dv_total.astype(jnp.bfloat16)
    for p in range(block_count):
        src = slice(p * block, (p + 1) * block)
        dst = slice((block_count - 1 - p) * block, (block_count - p) * block)
        dkdv_ref[dst, 0:HD] = dk[src]
        dkdv_ref[dst, HD : 2 * HD] = dv[src]


def slab_attention(mask, queries, output_grad, attn_output, key_value, slab_count):
    query_rows = queries.shape[0]
    key_rows = key_value.shape[0]
    vmem = pl.BlockSpec(memory_space=pltpu.VMEM)
    flops = 2 * query_rows * key_rows * HD * 5
    return pl.pallas_call(
        functools.partial(attention_kernel, slab_count, 1.0 / math.sqrt(HD)),
        out_shape=(
            jax.ShapeDtypeStruct((query_rows, HD), jnp.float32),
            jax.ShapeDtypeStruct((key_rows, 2 * HD), jnp.bfloat16),
        ),
        in_specs=[vmem] * 5,
        out_specs=(vmem, vmem),
        compiler_params=pltpu.CompilerParams(vmem_limit_bytes=48 * 1024 * 1024),
        cost_estimate=pl.CostEstimate(
            flops=flops,
            transcendentals=2 * query_rows * key_rows,
            bytes_accessed=key_rows * HD * 2 * 4,
        ),
    )(mask, queries, output_grad, attn_output, key_value)


def _pair_permute(value, distances):
    ctx_count, tp_count = lax.axis_size("ctx"), lax.axis_size("tp")
    pairs = [
        (c * tp_count + t, (c ^ distances[t % 2]) * tp_count + t)
        for c in range(ctx_count)
        for t in range(tp_count)
    ]
    return lax.ppermute(value, ("ctx", "tp"), pairs)


def gather_positions(me, distances, count):
    offset = me ^ jnp.arange(count, dtype=jnp.int32)
    return sum(((offset & d) != 0).astype(jnp.int32) << r for r, d in enumerate(distances))


def scatter_positions(me, distances, count):
    offset = me ^ jnp.arange(count, dtype=jnp.int32)
    top = len(distances) - 1
    return sum(((offset & d) == 0).astype(jnp.int32) << (top - r) for r, d in enumerate(distances))


def per_core(core, tables):
    return jnp.where(core == 0, tables[0], tables[1])


def concat_gather(x, orders):
    held = x
    for distances in zip(*orders):
        held = jnp.concatenate([held, _pair_permute(held, distances)], axis=0)
    return held


def halving_reduce(x, orders, wire=jnp.bfloat16):
    held = x
    for distances in zip(*orders):
        half = held.shape[0] // 2
        sent = _pair_permute(held[:half].astype(wire), distances)
        held = held[half:].astype(jnp.float32) + sent.astype(jnp.float32)
    return held


def tp_halving_reduce(x, order, wire=jnp.bfloat16):
    count = lax.axis_size("tp")
    held = x
    for distance in order:
        half = held.shape[0] // 2
        sent = lax.ppermute(
            held[:half].astype(wire), "tp", [(i, i ^ distance) for i in range(count)]
        )
        held = held[half:].astype(jnp.float32) + sent.astype(jnp.float32)
    return held


def xor_of_position(distances, count):
    position = jnp.arange(count, dtype=jnp.int32)
    return sum(((position >> r) & 1) * d for r, d in enumerate(distances))


def per_device(
    queries, key_states, value_states, attn_output, output_grad, block_map, w_query, w_key, w_value
):
    slab_rows, width = queries.shape
    ctx_count = lax.axis_size("ctx")
    me = lax.axis_index("ctx")
    tp_count = lax.axis_size("tp")
    me_tp = lax.axis_index("tp")
    core = me_tp % 2
    odd = me % 2
    low = odd == 0
    stacked = jnp.stack([queries, output_grad, attn_output, key_states, value_states])
    head_0, head_1 = stacked[:, :, :HD], stacked[:, :, HD : 2 * HD]
    kept = jnp.where(low, head_0, head_1)
    given = jnp.where(low, head_1, head_0)
    got = _pair_permute(given, (1, 1))
    both = jnp.where(low, jnp.concatenate([kept, got], 1), jnp.concatenate([got, kept], 1))
    pair_q, pair_do, pair_o, pair_k, pair_v = (both[i] for i in range(5))
    pair_kv = jnp.concatenate([pair_k, pair_v], axis=1)
    gathered = concat_gather(pair_kv, HEAD_GATHER_ORDERS)
    group_count = ctx_count // 2
    holder = me ^ per_core(core, [xor_of_position(o, group_count) for o in HEAD_GATHER_ORDERS])
    base = holder - holder % 2
    key_slabs = jnp.stack([base, base + 1], axis=1).reshape(-1) * slab_rows // BLK
    first = (me - odd) * slab_rows // BLK
    mask_rows = jnp.stack([block_map[first][key_slabs], block_map[first + 1][key_slabs]])
    mask = jnp.repeat(mask_rows.astype(jnp.float32), BLK, axis=1)
    mask = jnp.concatenate([mask, jnp.zeros((6, mask.shape[1]), jnp.float32)], axis=0)
    pair_dq, part_grads = slab_attention(mask, pair_q, pair_do, pair_o, gathered, 2)
    finished = halving_reduce(part_grads, HEAD_SCATTER_ORDERS).astype(jnp.bfloat16)
    pair_grads = jnp.concatenate([pair_dq.astype(jnp.bfloat16), finished], axis=1)
    lower, upper = pair_grads[:slab_rows], pair_grads[slab_rows:]
    mine = jnp.where(low, lower, upper)
    back = _pair_permute(jnp.where(low, upper, lower), (1, 1))
    first_head = jnp.where(low, mine, back)
    second_head = jnp.where(low, back, mine)
    own_grads = jnp.concatenate(
        [
            first_head[:, 0:HD], second_head[:, 0:HD],
            first_head[:, HD : 2 * HD], second_head[:, HD : 2 * HD],
            first_head[:, 2 * HD : 3 * HD], second_head[:, 2 * HD : 3 * HD],
        ],
        axis=1,
    )
    gather_at = per_core(core, [gather_positions(me, o, ctx_count) for o in GATHER_ORDERS])
    gradients = concat_gather(own_grads, GATHER_ORDERS)
    projections = jnp.concatenate([w_query, w_key, w_value], axis=1)
    term = lax.dot_general(
        gradients, projections, (((1,), (1,)), ((), ())), preferred_element_type=jnp.float32
    ).astype(jnp.bfloat16)
    tp_at = scatter_positions(me_tp, TP_ORDER, tp_count)
    owner = jnp.argsort(tp_at)
    per_owner = ctx_count // tp_count
    wanted = (owner[:, None] * per_owner + jnp.arange(per_owner)[None, :]).reshape(-1)
    source = gather_at[wanted]
    ordered = jnp.take(term.reshape(ctx_count, slab_rows, -1), source, axis=0)
    return tp_halving_reduce(ordered.reshape(ctx_count * slab_rows, -1), TP_ORDER).astype(
        jnp.bfloat16
    )


def solution(mesh):
    return jax.shard_map(
        per_device,
        mesh=mesh,
        in_specs=(
            P("ctx", "tp"),
            P("ctx", "tp"),
            P("ctx", "tp"),
            P("ctx", "tp"),
            P("ctx", "tp"),
            P(),
            P("ctx", "tp"),
            P("ctx", "tp"),
            P("ctx", "tp"),
        ),
        out_specs=P("tp", "ctx"),
        check_vma=False,
    )
```

```python
import functools
import math

import jax
import jax.numpy as jnp
from jax import lax
from jax.experimental import pallas as pl
from jax.experimental.pallas import tpu as pltpu
from jax.sharding import PartitionSpec as P

HD = 128
BLK = 128


NEG_FILL = -1e30
GATHER_ORDERS = ((4, 2, 16, 8, 1), (4, 16, 2, 1, 8))
SCATTER_ORDERS = tuple(tuple(reversed(order)) for order in GATHER_ORDERS)
HEAD_GATHER_ORDERS = ((4, 2, 16, 8), (4, 16, 2, 8))
HEAD_SCATTER_ORDERS = tuple(tuple(reversed(order)) for order in HEAD_GATHER_ORDERS)
TP_ORDER = (1, 4, 8, 2)


def _nt(a, b):
    return lax.dot_general(a, b, (((1,), (1,)), ((), ())), preferred_element_type=jnp.float32)


def _tn(a, b):
    return lax.dot_general(a, b, (((0,), (0,)), ((), ())), preferred_element_type=jnp.float32)


def attention_kernel(slab_count, score_scale, mask_ref, q_ref, do_ref, o_ref, kv_ref, dq_ref, dkdv_ref):
    key_rows = kv_ref.shape[0]
    rows = q_ref.shape[0] // slab_count
    block = rows * slab_count
    block_count = key_rows // block
    k_h = kv_ref[:, 0:HD]
    dk_total = jnp.zeros((key_rows, HD), jnp.float32)
    dv_total = jnp.zeros((key_rows, HD), jnp.float32)
    for a in range(slab_count):
        mine = slice(a * rows, (a + 1) * rows)
        allowed = mask_ref[a : a + 1, :] > 0
        q_h = q_ref[mine, :]
        do_h = do_ref[mine, :]
        scores = _nt(q_h, k_h) * score_scale
        masked = jnp.where(allowed, scores, NEG_FILL)
        row_max = jnp.max(masked, axis=1, keepdims=True)
        row_sum = jnp.sum(jnp.where(allowed, jnp.exp(masked - row_max), 0.0), axis=1, keepdims=True)
        log_total = row_max + jnp.log(row_sum)
        probs = jnp.where(allowed, jnp.exp(masked - log_total), 0.0)
        row_delta = jnp.sum(
            do_h.astype(jnp.float32) * o_ref[mine, :].astype(jnp.float32), axis=1, keepdims=True
        )
        dprobs = _nt(do_h, kv_ref[:, HD : 2 * HD])
        score_gradient = (probs * (dprobs - row_delta) * score_scale).astype(jnp.bfloat16)
        dq_ref[mine, :] = jnp.dot(score_gradient, k_h, preferred_element_type=jnp.float32)
        dk_total = dk_total + _tn(score_gradient, q_h)
        dv_total = dv_total + _tn(probs.astype(jnp.bfloat16), do_h)
    dk = dk_total.astype(jnp.bfloat16)
    dv = dv_total.astype(jnp.bfloat16)
    for p in range(block_count):
        src = slice(p * block, (p + 1) * block)
        dst = slice((block_count - 1 - p) * block, (block_count - p) * block)
        dkdv_ref[dst, 0:HD] = dk[src]
        dkdv_ref[dst, HD : 2 * HD] = dv[src]


def slab_attention(mask, queries, output_grad, attn_output, key_value, slab_count):
    query_rows = queries.shape[0]
    key_rows = key_value.shape[0]
    vmem = pl.BlockSpec(memory_space=pltpu.VMEM)
    flops = 2 * query_rows * key_rows * HD * 5
    return pl.pallas_call(
        functools.partial(attention_kernel, slab_count, 1.0 / math.sqrt(HD)),
        out_shape=(
            jax.ShapeDtypeStruct((query_rows, HD), jnp.float32),
            jax.ShapeDtypeStruct((key_rows, 2 * HD), jnp.bfloat16),
        ),
        in_specs=[vmem] * 5,
        out_specs=(vmem, vmem),
        compiler_params=pltpu.CompilerParams(vmem_limit_bytes=48 * 1024 * 1024),
        cost_estimate=pl.CostEstimate(
            flops=flops,
            transcendentals=2 * query_rows * key_rows,
            bytes_accessed=key_rows * HD * 2 * 4,
        ),
    )(mask, queries, output_grad, attn_output, key_value)


def _pair_permute(value, distances):
    ctx_count, tp_count = lax.axis_size("ctx"), lax.axis_size("tp")
    pairs = [
        (c * tp_count + t, (c ^ distances[t % 2]) * tp_count + t)
        for c in range(ctx_count)
        for t in range(tp_count)
    ]
    return lax.ppermute(value, ("ctx", "tp"), pairs)


def gather_positions(me, distances, count):
    offset = me ^ jnp.arange(count, dtype=jnp.int32)
    return sum(((offset & d) != 0).astype(jnp.int32) << r for r, d in enumerate(distances))


def scatter_positions(me, distances, count):
    offset = me ^ jnp.arange(count, dtype=jnp.int32)
    top = len(distances) - 1
    return sum(((offset & d) == 0).astype(jnp.int32) << (top - r) for r, d in enumerate(distances))


def per_core(core, tables):
    return jnp.where(core == 0, tables[0], tables[1])


def concat_gather(x, orders):
    held = x
    for distances in zip(*orders):
        held = jnp.concatenate([held, _pair_permute(held, distances)], axis=0)
    return held


def halving_reduce(x, orders, wire=jnp.bfloat16):
    held = x
    for distances in zip(*orders):
        half = held.shape[0] // 2
        sent = _pair_permute(held[:half].astype(wire), distances)
        held = held[half:].astype(jnp.float32) + sent.astype(jnp.float32)
    return held


def tp_halving_reduce(x, order, wire=jnp.bfloat16):
    count = lax.axis_size("tp")
    held = x
    for distance in order:
        half = held.shape[0] // 2
        sent = lax.ppermute(
            held[:half].astype(wire), "tp", [(i, i ^ distance) for i in range(count)]
        )
        held = held[half:].astype(jnp.float32) + sent.astype(jnp.float32)
    return held


def xor_of_position(distances, count):
    position = jnp.arange(count, dtype=jnp.int32)
    return sum(((position >> r) & 1) * d for r, d in enumerate(distances))


def per_device(
    queries, key_states, value_states, attn_output, output_grad, block_map, w_query, w_key, w_value
):
    slab_rows, width = queries.shape
    ctx_count = lax.axis_size("ctx")
    me = lax.axis_index("ctx")
    tp_count = lax.axis_size("tp")
    me_tp = lax.axis_index("tp")
    core = me_tp % 2
    odd = me % 2
    low = odd == 0
    arrays = (queries, output_grad, attn_output, key_states, value_states)
    kept = jnp.concatenate([lax.dynamic_slice_in_dim(x, odd * HD, HD, 1) for x in arrays], axis=1)
    given = jnp.concatenate(
        [lax.dynamic_slice_in_dim(x, (1 - odd) * HD, HD, 1) for x in arrays], axis=1
    )
    got = _pair_permute(given, (1, 1))
    both = jnp.where(low, jnp.concatenate([kept, got], 0), jnp.concatenate([got, kept], 0))
    pair_q, pair_do, pair_o = both[:, 0:HD], both[:, HD : 2 * HD], both[:, 2 * HD : 3 * HD]
    pair_kv = both[:, 3 * HD : 5 * HD]
    gathered = concat_gather(pair_kv, HEAD_GATHER_ORDERS)
    group_count = ctx_count // 2
    holder = me ^ per_core(core, [xor_of_position(o, group_count) for o in HEAD_GATHER_ORDERS])
    base = holder - holder % 2
    key_slabs = jnp.stack([base, base + 1], axis=1).reshape(-1) * slab_rows // BLK
    first = (me - odd) * slab_rows // BLK
    mask_rows = jnp.stack([block_map[first][key_slabs], block_map[first + 1][key_slabs]])
    mask = jnp.repeat(mask_rows.astype(jnp.float32), BLK, axis=1)
    mask = jnp.concatenate([mask, jnp.zeros((6, mask.shape[1]), jnp.float32)], axis=0)
    pair_dq, part_grads = slab_attention(mask, pair_q, pair_do, pair_o, gathered, 2)
    finished = halving_reduce(part_grads, HEAD_SCATTER_ORDERS).astype(jnp.bfloat16)
    pair_grads = jnp.concatenate([pair_dq.astype(jnp.bfloat16), finished], axis=1)
    lower, upper = pair_grads[:slab_rows], pair_grads[slab_rows:]
    mine = jnp.where(low, lower, upper)
    back = _pair_permute(jnp.where(low, upper, lower), (1, 1))
    first_head = jnp.where(low, mine, back)
    second_head = jnp.where(low, back, mine)
    own_grads = jnp.concatenate(
        [
            first_head[:, 0:HD], second_head[:, 0:HD],
            first_head[:, HD : 2 * HD], second_head[:, HD : 2 * HD],
            first_head[:, 2 * HD : 3 * HD], second_head[:, 2 * HD : 3 * HD],
        ],
        axis=1,
    )
    gather_at = per_core(core, [gather_positions(me, o, ctx_count) for o in GATHER_ORDERS])
    held = concat_gather(own_grads, tuple(order[:-1] for order in GATHER_ORDERS))
    other = _pair_permute(held, tuple(order[-1] for order in GATHER_ORDERS))
    projections = jnp.concatenate([w_query, w_key, w_value], axis=1)

    def project(rows):
        return lax.dot_general(
            rows, projections, (((1,), (1,)), ((), ())), preferred_element_type=jnp.float32
        ).astype(jnp.bfloat16)

    term = jnp.concatenate([project(held), project(other)], axis=0)
    tp_at = scatter_positions(me_tp, TP_ORDER, tp_count)
    owner = jnp.argsort(tp_at)
    per_owner = ctx_count // tp_count
    wanted = (owner[:, None] * per_owner + jnp.arange(per_owner)[None, :]).reshape(-1)
    source = gather_at[wanted]
    ordered = jnp.take(term.reshape(ctx_count, slab_rows, -1), source, axis=0)
    return tp_halving_reduce(ordered.reshape(ctx_count * slab_rows, -1), TP_ORDER).astype(
        jnp.bfloat16
    )


def solution(mesh):
    return jax.shard_map(
        per_device,
        mesh=mesh,
        in_specs=(
            P("ctx", "tp"),
            P("ctx", "tp"),
            P("ctx", "tp"),
            P("ctx", "tp"),
            P("ctx", "tp"),
            P(),
            P("ctx", "tp"),
            P("ctx", "tp"),
            P("ctx", "tp"),
        ),
        out_specs=P("tp", "ctx"),
        check_vma=False,
    )
```

```python
import functools
import math

import jax
import jax.numpy as jnp
from jax import lax
from jax.experimental import pallas as pl
from jax.experimental.pallas import tpu as pltpu
from jax.sharding import PartitionSpec as P

HD = 128
BLK = 128


NEG_FILL = -1e30
GATHER_ORDERS = ((4, 2, 16, 8, 1), (4, 16, 2, 1, 8))
SCATTER_ORDERS = tuple(tuple(reversed(order)) for order in GATHER_ORDERS)
HEAD_GATHER_ORDERS = ((4, 2, 16, 8), (4, 16, 2, 8))
HEAD_SCATTER_ORDERS = tuple(tuple(reversed(order)) for order in HEAD_GATHER_ORDERS)
TP_ORDERS = ((1, 4, 12, 2), (1, 12, 4, 2))


def _nt(a, b):
    return lax.dot_general(a, b, (((1,), (1,)), ((), ())), preferred_element_type=jnp.float32)


def _tn(a, b):
    return lax.dot_general(a, b, (((0,), (0,)), ((), ())), preferred_element_type=jnp.float32)


def attention_kernel(slab_count, score_scale, mask_ref, q_ref, do_ref, o_ref, kv_ref, dq_ref, dkdv_ref):
    key_rows = kv_ref.shape[0]
    rows = q_ref.shape[0] // slab_count
    block = rows * slab_count
    block_count = key_rows // block
    k_h = kv_ref[:, 0:HD]
    dk_total = jnp.zeros((key_rows, HD), jnp.float32)
    dv_total = jnp.zeros((key_rows, HD), jnp.float32)
    for a in range(slab_count):
        mine = slice(a * rows, (a + 1) * rows)
        allowed = mask_ref[a : a + 1, :] > 0
        q_h = q_ref[mine, :]
        do_h = do_ref[mine, :]
        scores = _nt(q_h, k_h) * score_scale
        masked = jnp.where(allowed, scores, NEG_FILL)
        row_max = jnp.max(masked, axis=1, keepdims=True)
        row_sum = jnp.sum(jnp.where(allowed, jnp.exp(masked - row_max), 0.0), axis=1, keepdims=True)
        log_total = row_max + jnp.log(row_sum)
        probs = jnp.where(allowed, jnp.exp(masked - log_total), 0.0)
        row_delta = jnp.sum(
            do_h.astype(jnp.float32) * o_ref[mine, :].astype(jnp.float32), axis=1, keepdims=True
        )
        dprobs = _nt(do_h, kv_ref[:, HD : 2 * HD])
        score_gradient = (probs * (dprobs - row_delta) * score_scale).astype(jnp.bfloat16)
        dq_ref[mine, :] = jnp.dot(score_gradient, k_h, preferred_element_type=jnp.float32)
        dk_total = dk_total + _tn(score_gradient, q_h)
        dv_total = dv_total + _tn(probs.astype(jnp.bfloat16), do_h)
    dk = dk_total.astype(jnp.bfloat16)
    dv = dv_total.astype(jnp.bfloat16)
    for p in range(block_count):
        src = slice(p * block, (p + 1) * block)
        dst = slice((block_count - 1 - p) * block, (block_count - p) * block)
        dkdv_ref[dst, 0:HD] = dk[src]
        dkdv_ref[dst, HD : 2 * HD] = dv[src]


def slab_attention(mask, queries, output_grad, attn_output, key_value, slab_count):
    query_rows = queries.shape[0]
    key_rows = key_value.shape[0]
    vmem = pl.BlockSpec(memory_space=pltpu.VMEM)
    flops = 2 * query_rows * key_rows * HD * 5
    return pl.pallas_call(
        functools.partial(attention_kernel, slab_count, 1.0 / math.sqrt(HD)),
        out_shape=(
            jax.ShapeDtypeStruct((query_rows, HD), jnp.float32),
            jax.ShapeDtypeStruct((key_rows, 2 * HD), jnp.bfloat16),
        ),
        in_specs=[vmem] * 5,
        out_specs=(vmem, vmem),
        compiler_params=pltpu.CompilerParams(vmem_limit_bytes=48 * 1024 * 1024),
        cost_estimate=pl.CostEstimate(
            flops=flops,
            transcendentals=2 * query_rows * key_rows,
            bytes_accessed=key_rows * HD * 2 * 4,
        ),
    )(mask, queries, output_grad, attn_output, key_value)


def _pair_permute(value, distances):
    ctx_count, tp_count = lax.axis_size("ctx"), lax.axis_size("tp")
    pairs = [
        (c * tp_count + t, (c ^ distances[t % 2]) * tp_count + t)
        for c in range(ctx_count)
        for t in range(tp_count)
    ]
    return lax.ppermute(value, ("ctx", "tp"), pairs)


def gather_positions(me, distances, count):
    offset = me ^ jnp.arange(count, dtype=jnp.int32)
    return sum(((offset & d) != 0).astype(jnp.int32) << r for r, d in enumerate(distances))


def _coefficient_masks(distances):
    width = max(distances).bit_length()
    masks = []
    for r in range(len(distances)):
        for m in range(1 << width):
            if all(bin(d & m).count("1") % 2 == (r == s) for s, d in enumerate(distances)):
                masks.append(m)
                break
    return masks


def scatter_positions(me, distances, count):
    offset = me ^ jnp.arange(count, dtype=jnp.int32)
    top = len(distances) - 1
    return sum(
        ((lax.population_count(offset & m) & 1) == 0).astype(jnp.int32) << (top - r)
        for r, m in enumerate(_coefficient_masks(distances))
    )


def per_core(core, tables):
    return jnp.where(core == 0, tables[0], tables[1])


def concat_gather(x, orders):
    held = x
    for distances in zip(*orders):
        held = jnp.concatenate([held, _pair_permute(held, distances)], axis=0)
    return held


def halving_reduce(x, orders, wire=jnp.bfloat16):
    held = x
    for distances in zip(*orders):
        half = held.shape[0] // 2
        sent = _pair_permute(held[:half].astype(wire), distances)
        held = held[half:].astype(jnp.float32) + sent.astype(jnp.float32)
    return held


def tp_positions(me, core, count):
    first, rest = TP_ORDERS[0][0], [order[1:] for order in TP_ORDERS]
    assert all(order[0] == first for order in TP_ORDERS)
    offset = me ^ jnp.arange(count, dtype=jnp.int32)
    sent = (lax.population_count(offset & _coefficient_masks(TP_ORDERS[0])[0]) & 1) == 1

    def later(off, order):
        masks = _coefficient_masks((first,) + tuple(order))[1:]
        top = len(masks) - 1
        return sum(
            ((lax.population_count(off & m) & 1) == 0).astype(jnp.int32) << (top - r)
            for r, m in enumerate(masks)
        )

    mine = per_core(core, [later(offset, o) for o in rest])
    theirs = per_core(core, [later(offset ^ first, o) for o in reversed(rest)])
    return jnp.where(sent, theirs, count // 2 + mine)


def tp_halving_reduce(x, orders, wire=jnp.bfloat16):
    count = lax.axis_size("tp")
    held = x
    for distances in zip(*orders):
        half = held.shape[0] // 2
        pairs = [(i, i ^ distances[i % 2]) for i in range(count)]
        sent = lax.ppermute(held[:half].astype(wire), "tp", pairs)
        held = held[half:].astype(jnp.float32) + sent.astype(jnp.float32)
    return held


def xor_of_position(distances, count):
    position = jnp.arange(count, dtype=jnp.int32)
    return sum(((position >> r) & 1) * d for r, d in enumerate(distances))


def per_device(
    queries, key_states, value_states, attn_output, output_grad, block_map, w_query, w_key, w_value
):
    slab_rows, width = queries.shape
    ctx_count = lax.axis_size("ctx")
    me = lax.axis_index("ctx")
    tp_count = lax.axis_size("tp")
    me_tp = lax.axis_index("tp")
    core = me_tp % 2
    odd = me % 2
    low = odd == 0
    arrays = (queries, output_grad, attn_output, key_states, value_states)
    kept = jnp.concatenate([lax.dynamic_slice_in_dim(x, odd * HD, HD, 1) for x in arrays], axis=1)
    given = jnp.concatenate(
        [lax.dynamic_slice_in_dim(x, (1 - odd) * HD, HD, 1) for x in arrays], axis=1
    )
    got = _pair_permute(given, (1, 1))
    both = jnp.where(low, jnp.concatenate([kept, got], 0), jnp.concatenate([got, kept], 0))
    pair_q, pair_do, pair_o = both[:, 0:HD], both[:, HD : 2 * HD], both[:, 2 * HD : 3 * HD]
    pair_kv = both[:, 3 * HD : 5 * HD]
    gathered = concat_gather(pair_kv, HEAD_GATHER_ORDERS)
    group_count = ctx_count // 2
    holder = me ^ per_core(core, [xor_of_position(o, group_count) for o in HEAD_GATHER_ORDERS])
    base = holder - holder % 2
    key_slabs = jnp.stack([base, base + 1], axis=1).reshape(-1) * slab_rows // BLK
    first = (me - odd) * slab_rows // BLK
    mask_rows = jnp.stack([block_map[first][key_slabs], block_map[first + 1][key_slabs]])
    mask = jnp.repeat(mask_rows.astype(jnp.float32), BLK, axis=1)
    mask = jnp.concatenate([mask, jnp.zeros((6, mask.shape[1]), jnp.float32)], axis=0)
    pair_dq, part_grads = slab_attention(mask, pair_q, pair_do, pair_o, gathered, 2)
    finished = halving_reduce(part_grads, HEAD_SCATTER_ORDERS).astype(jnp.bfloat16)
    pair_grads = jnp.concatenate([pair_dq.astype(jnp.bfloat16), finished], axis=1)
    lower, upper = pair_grads[:slab_rows], pair_grads[slab_rows:]
    mine = jnp.where(low, lower, upper)
    back = _pair_permute(jnp.where(low, upper, lower), (1, 1))
    first_head = jnp.where(low, mine, back)
    second_head = jnp.where(low, back, mine)
    own_grads = jnp.concatenate(
        [
            first_head[:, 0:HD], second_head[:, 0:HD],
            first_head[:, HD : 2 * HD], second_head[:, HD : 2 * HD],
            first_head[:, 2 * HD : 3 * HD], second_head[:, 2 * HD : 3 * HD],
        ],
        axis=1,
    )
    gather_at = per_core(core, [gather_positions(me, o, ctx_count) for o in GATHER_ORDERS])
    held = concat_gather(own_grads, tuple(order[:-1] for order in GATHER_ORDERS))
    other = _pair_permute(held, tuple(order[-1] for order in GATHER_ORDERS))
    projections = jnp.concatenate([w_query, w_key, w_value], axis=1)

    def project(rows):
        return lax.dot_general(
            rows, projections, (((1,), (1,)), ((), ())), preferred_element_type=jnp.float32
        ).astype(jnp.bfloat16)

    term = jnp.concatenate([project(held), project(other)], axis=0)
    tp_at = tp_positions(me_tp, core, tp_count)
    owner = jnp.argsort(tp_at)
    per_owner = ctx_count // tp_count
    wanted = (owner[:, None] * per_owner + jnp.arange(per_owner)[None, :]).reshape(-1)
    source = gather_at[wanted]
    ordered = jnp.take(term.reshape(ctx_count, slab_rows, -1), source, axis=0)
    return tp_halving_reduce(ordered.reshape(ctx_count * slab_rows, -1), TP_ORDERS).astype(
        jnp.bfloat16
    )


def solution(mesh):
    return jax.shard_map(
        per_device,
        mesh=mesh,
        in_specs=(
            P("ctx", "tp"),
            P("ctx", "tp"),
            P("ctx", "tp"),
            P("ctx", "tp"),
            P("ctx", "tp"),
            P(),
            P("ctx", "tp"),
            P("ctx", "tp"),
            P("ctx", "tp"),
        ),
        out_specs=P("tp", "ctx"),
        check_vma=False,
    )
```

```python
import functools
import math

import jax
import jax.numpy as jnp
from jax import lax
from jax.experimental import pallas as pl
from jax.experimental.pallas import tpu as pltpu
from jax.sharding import PartitionSpec as P

HD = 128
BLK = 128


NEG_FILL = -1e30
GATHER_ORDERS = ((4, 2, 24, 8, 1), (4, 24, 2, 1, 8))
SCATTER_ORDERS = tuple(tuple(reversed(order)) for order in GATHER_ORDERS)
HEAD_GATHER_ORDERS = ((4, 2, 24, 8), (4, 24, 2, 8))
HEAD_SCATTER_ORDERS = tuple(tuple(reversed(order)) for order in HEAD_GATHER_ORDERS)
TP_ORDERS = ((1, 4, 12, 2), (1, 12, 4, 2))


def _nt(a, b):
    return lax.dot_general(a, b, (((1,), (1,)), ((), ())), preferred_element_type=jnp.float32)


def _tn(a, b):
    return lax.dot_general(a, b, (((0,), (0,)), ((), ())), preferred_element_type=jnp.float32)


def attention_kernel(slab_count, score_scale, mask_ref, q_ref, do_ref, o_ref, kv_ref, dq_ref, dkdv_ref):
    key_rows = kv_ref.shape[0]
    rows = q_ref.shape[0] // slab_count
    block = rows * slab_count
    block_count = key_rows // block
    k_h = kv_ref[:, 0:HD]
    dk_total = jnp.zeros((key_rows, HD), jnp.float32)
    dv_total = jnp.zeros((key_rows, HD), jnp.float32)
    for a in range(slab_count):
        mine = slice(a * rows, (a + 1) * rows)
        allowed = mask_ref[a : a + 1, :] > 0
        q_h = q_ref[mine, :]
        do_h = do_ref[mine, :]
        scores = _nt(q_h, k_h) * score_scale
        masked = jnp.where(allowed, scores, NEG_FILL)
        row_max = jnp.max(masked, axis=1, keepdims=True)
        row_sum = jnp.sum(jnp.where(allowed, jnp.exp(masked - row_max), 0.0), axis=1, keepdims=True)
        log_total = row_max + jnp.log(row_sum)
        probs = jnp.where(allowed, jnp.exp(masked - log_total), 0.0)
        row_delta = jnp.sum(
            do_h.astype(jnp.float32) * o_ref[mine, :].astype(jnp.float32), axis=1, keepdims=True
        )
        dprobs = _nt(do_h, kv_ref[:, HD : 2 * HD])
        score_gradient = (probs * (dprobs - row_delta) * score_scale).astype(jnp.bfloat16)
        dq_ref[mine, :] = jnp.dot(score_gradient, k_h, preferred_element_type=jnp.float32)
        dk_total = dk_total + _tn(score_gradient, q_h)
        dv_total = dv_total + _tn(probs.astype(jnp.bfloat16), do_h)
    dk = dk_total.astype(jnp.bfloat16)
    dv = dv_total.astype(jnp.bfloat16)
    for p in range(block_count):
        src = slice(p * block, (p + 1) * block)
        dst = slice((block_count - 1 - p) * block, (block_count - p) * block)
        dkdv_ref[dst, 0:HD] = dk[src]
        dkdv_ref[dst, HD : 2 * HD] = dv[src]


def slab_attention(mask, queries, output_grad, attn_output, key_value, slab_count):
    query_rows = queries.shape[0]
    key_rows = key_value.shape[0]
    vmem = pl.BlockSpec(memory_space=pltpu.VMEM)
    flops = 2 * query_rows * key_rows * HD * 5
    return pl.pallas_call(
        functools.partial(attention_kernel, slab_count, 1.0 / math.sqrt(HD)),
        out_shape=(
            jax.ShapeDtypeStruct((query_rows, HD), jnp.float32),
            jax.ShapeDtypeStruct((key_rows, 2 * HD), jnp.bfloat16),
        ),
        in_specs=[vmem] * 5,
        out_specs=(vmem, vmem),
        compiler_params=pltpu.CompilerParams(vmem_limit_bytes=48 * 1024 * 1024),
        cost_estimate=pl.CostEstimate(
            flops=flops,
            transcendentals=2 * query_rows * key_rows,
            bytes_accessed=key_rows * HD * 2 * 4,
        ),
    )(mask, queries, output_grad, attn_output, key_value)


def _pair_permute(value, distances):
    ctx_count, tp_count = lax.axis_size("ctx"), lax.axis_size("tp")
    pairs = [
        (c * tp_count + t, (c ^ distances[t % 2]) * tp_count + t)
        for c in range(ctx_count)
        for t in range(tp_count)
    ]
    return lax.ppermute(value, ("ctx", "tp"), pairs)


def gather_positions(me, distances, count):
    offset = me ^ jnp.arange(count, dtype=jnp.int32)
    return sum(
        (lax.population_count(offset & m) & 1) << r
        for r, m in enumerate(_coefficient_masks(distances))
    )


def _coefficient_masks(distances):
    width = max(distances).bit_length()
    masks = []
    for r in range(len(distances)):
        for m in range(1 << width):
            if all(bin(d & m).count("1") % 2 == (r == s) for s, d in enumerate(distances)):
                masks.append(m)
                break
    return masks


def scatter_positions(me, distances, count):
    offset = me ^ jnp.arange(count, dtype=jnp.int32)
    top = len(distances) - 1
    return sum(
        ((lax.population_count(offset & m) & 1) == 0).astype(jnp.int32) << (top - r)
        for r, m in enumerate(_coefficient_masks(distances))
    )


def per_core(core, tables):
    return jnp.where(core == 0, tables[0], tables[1])


def concat_gather(x, orders):
    held = x
    for distances in zip(*orders):
        held = jnp.concatenate([held, _pair_permute(held, distances)], axis=0)
    return held


def halving_reduce(x, orders, wire=jnp.bfloat16):
    held = x
    for distances in zip(*orders):
        half = held.shape[0] // 2
        sent = _pair_permute(held[:half].astype(wire), distances)
        held = held[half:].astype(jnp.float32) + sent.astype(jnp.float32)
    return held


def tp_positions(me, core, count):
    first, rest = TP_ORDERS[0][0], [order[1:] for order in TP_ORDERS]
    assert all(order[0] == first for order in TP_ORDERS)
    offset = me ^ jnp.arange(count, dtype=jnp.int32)
    sent = (lax.population_count(offset & _coefficient_masks(TP_ORDERS[0])[0]) & 1) == 1

    def later(off, order):
        masks = _coefficient_masks((first,) + tuple(order))[1:]
        top = len(masks) - 1
        return sum(
            ((lax.population_count(off & m) & 1) == 0).astype(jnp.int32) << (top - r)
            for r, m in enumerate(masks)
        )

    mine = per_core(core, [later(offset, o) for o in rest])
    theirs = per_core(core, [later(offset ^ first, o) for o in reversed(rest)])
    return jnp.where(sent, theirs, count // 2 + mine)


def tp_halving_reduce(x, orders, wire=jnp.bfloat16):
    count = lax.axis_size("tp")
    held = x
    for distances in zip(*orders):
        half = held.shape[0] // 2
        pairs = [(i, i ^ distances[i % 2]) for i in range(count)]
        sent = lax.ppermute(held[:half].astype(wire), "tp", pairs)
        held = held[half:].astype(jnp.float32) + sent.astype(jnp.float32)
    return held


def xor_of_position(distances, count):
    position = jnp.arange(count, dtype=jnp.int32)
    total = jnp.zeros_like(position)
    for r, d in enumerate(distances):
        total = total ^ (((position >> r) & 1) * d)
    return total


def per_device(
    queries, key_states, value_states, attn_output, output_grad, block_map, w_query, w_key, w_value
):
    slab_rows, width = queries.shape
    ctx_count = lax.axis_size("ctx")
    me = lax.axis_index("ctx")
    tp_count = lax.axis_size("tp")
    me_tp = lax.axis_index("tp")
    core = me_tp % 2
    odd = me % 2
    low = odd == 0
    arrays = (queries, output_grad, attn_output, key_states, value_states)
    kept = jnp.concatenate([lax.dynamic_slice_in_dim(x, odd * HD, HD, 1) for x in arrays], axis=1)
    given = jnp.concatenate(
        [lax.dynamic_slice_in_dim(x, (1 - odd) * HD, HD, 1) for x in arrays], axis=1
    )
    got = _pair_permute(given, (1, 1))
    both = jnp.where(low, jnp.concatenate([kept, got], 0), jnp.concatenate([got, kept], 0))
    pair_q, pair_do, pair_o = both[:, 0:HD], both[:, HD : 2 * HD], both[:, 2 * HD : 3 * HD]
    pair_kv = both[:, 3 * HD : 5 * HD]
    gathered = concat_gather(pair_kv, HEAD_GATHER_ORDERS)
    group_count = ctx_count // 2
    holder = me ^ per_core(core, [xor_of_position(o, group_count) for o in HEAD_GATHER_ORDERS])
    base = holder - holder % 2
    key_slabs = jnp.stack([base, base + 1], axis=1).reshape(-1) * slab_rows // BLK
    first = (me - odd) * slab_rows // BLK
    mask_rows = jnp.stack([block_map[first][key_slabs], block_map[first + 1][key_slabs]])
    mask = jnp.repeat(mask_rows.astype(jnp.float32), BLK, axis=1)
    mask = jnp.concatenate([mask, jnp.zeros((6, mask.shape[1]), jnp.float32)], axis=0)
    pair_dq, part_grads = slab_attention(mask, pair_q, pair_do, pair_o, gathered, 2)
    finished = halving_reduce(part_grads, HEAD_SCATTER_ORDERS).astype(jnp.bfloat16)
    pair_grads = jnp.concatenate([pair_dq.astype(jnp.bfloat16), finished], axis=1)
    lower, upper = pair_grads[:slab_rows], pair_grads[slab_rows:]
    mine = jnp.where(low, lower, upper)
    back = _pair_permute(jnp.where(low, upper, lower), (1, 1))
    first_head = jnp.where(low, mine, back)
    second_head = jnp.where(low, back, mine)
    own_grads = jnp.concatenate(
        [
            first_head[:, 0:HD], second_head[:, 0:HD],
            first_head[:, HD : 2 * HD], second_head[:, HD : 2 * HD],
            first_head[:, 2 * HD : 3 * HD], second_head[:, 2 * HD : 3 * HD],
        ],
        axis=1,
    )
    gather_at = per_core(core, [gather_positions(me, o, ctx_count) for o in GATHER_ORDERS])
    held = concat_gather(own_grads, tuple(order[:-1] for order in GATHER_ORDERS))
    other = _pair_permute(held, tuple(order[-1] for order in GATHER_ORDERS))
    projections = jnp.concatenate([w_query, w_key, w_value], axis=1)

    def project(rows):
        return lax.dot_general(
            rows, projections, (((1,), (1,)), ((), ())), preferred_element_type=jnp.float32
        ).astype(jnp.bfloat16)

    term = jnp.concatenate([project(held), project(other)], axis=0)
    tp_at = tp_positions(me_tp, core, tp_count)
    owner = jnp.argsort(tp_at)
    per_owner = ctx_count // tp_count
    wanted = (owner[:, None] * per_owner + jnp.arange(per_owner)[None, :]).reshape(-1)
    source = gather_at[wanted]
    ordered = jnp.take(term.reshape(ctx_count, slab_rows, -1), source, axis=0)
    return tp_halving_reduce(ordered.reshape(ctx_count * slab_rows, -1), TP_ORDERS).astype(
        jnp.bfloat16
    )


def solution(mesh):
    return jax.shard_map(
        per_device,
        mesh=mesh,
        in_specs=(
            P("ctx", "tp"),
            P("ctx", "tp"),
            P("ctx", "tp"),
            P("ctx", "tp"),
            P("ctx", "tp"),
            P(),
            P("ctx", "tp"),
            P("ctx", "tp"),
            P("ctx", "tp"),
        ),
        out_specs=P("tp", "ctx"),
        check_vma=False,
    )
```

```python
import functools
import math

import jax
import jax.numpy as jnp
from jax import lax
from jax.experimental import pallas as pl
from jax.experimental.pallas import tpu as pltpu
from jax.sharding import PartitionSpec as P

HD = 128
BLK = 128


NEG_FILL = -1e30
GATHER_ORDERS = ((4, 2, 16, 8, 1), (4, 16, 2, 1, 8))
SCATTER_ORDERS = tuple(tuple(reversed(order)) for order in GATHER_ORDERS)
HEAD_GATHER_ORDERS = ((4, 2, 8, 16), (4, 16, 8, 2))
HEAD_SCATTER_ORDERS = tuple(tuple(reversed(order)) for order in HEAD_GATHER_ORDERS)
TP_ORDERS = ((1, 4, 12, 2), (1, 12, 4, 2))


def _nt(a, b):
    return lax.dot_general(a, b, (((1,), (1,)), ((), ())), preferred_element_type=jnp.float32)


def _tn(a, b):
    return lax.dot_general(a, b, (((0,), (0,)), ((), ())), preferred_element_type=jnp.float32)


def attention_kernel(slab_count, score_scale, mask_ref, q_ref, do_ref, o_ref, kv_ref, dq_ref, dkdv_ref):
    key_rows = kv_ref.shape[0]
    rows = q_ref.shape[0] // slab_count
    block = rows * slab_count
    block_count = key_rows // block
    k_h = kv_ref[:, 0:HD]
    dk_total = jnp.zeros((key_rows, HD), jnp.float32)
    dv_total = jnp.zeros((key_rows, HD), jnp.float32)
    for a in range(slab_count):
        mine = slice(a * rows, (a + 1) * rows)
        allowed = mask_ref[a : a + 1, :] > 0
        q_h = q_ref[mine, :]
        do_h = do_ref[mine, :]
        scores = _nt(q_h, k_h) * score_scale
        masked = jnp.where(allowed, scores, NEG_FILL)
        row_max = jnp.max(masked, axis=1, keepdims=True)
        row_sum = jnp.sum(jnp.where(allowed, jnp.exp(masked - row_max), 0.0), axis=1, keepdims=True)
        log_total = row_max + jnp.log(row_sum)
        probs = jnp.where(allowed, jnp.exp(masked - log_total), 0.0)
        row_delta = jnp.sum(
            do_h.astype(jnp.float32) * o_ref[mine, :].astype(jnp.float32), axis=1, keepdims=True
        )
        dprobs = _nt(do_h, kv_ref[:, HD : 2 * HD])
        score_gradient = (probs * (dprobs - row_delta) * score_scale).astype(jnp.bfloat16)
        dq_ref[mine, :] = jnp.dot(score_gradient, k_h, preferred_element_type=jnp.float32)
        dk_total = dk_total + _tn(score_gradient, q_h)
        dv_total = dv_total + _tn(probs.astype(jnp.bfloat16), do_h)
    dk = dk_total.astype(jnp.bfloat16)
    dv = dv_total.astype(jnp.bfloat16)
    for p in range(block_count):
        src = slice(p * block, (p + 1) * block)
        dst = slice((block_count - 1 - p) * block, (block_count - p) * block)
        dkdv_ref[dst, 0:HD] = dk[src]
        dkdv_ref[dst, HD : 2 * HD] = dv[src]


def slab_attention(mask, queries, output_grad, attn_output, key_value, slab_count):
    query_rows = queries.shape[0]
    key_rows = key_value.shape[0]
    vmem = pl.BlockSpec(memory_space=pltpu.VMEM)
    flops = 2 * query_rows * key_rows * HD * 5
    return pl.pallas_call(
        functools.partial(attention_kernel, slab_count, 1.0 / math.sqrt(HD)),
        out_shape=(
            jax.ShapeDtypeStruct((query_rows, HD), jnp.float32),
            jax.ShapeDtypeStruct((key_rows, 2 * HD), jnp.bfloat16),
        ),
        in_specs=[vmem] * 5,
        out_specs=(vmem, vmem),
        compiler_params=pltpu.CompilerParams(vmem_limit_bytes=48 * 1024 * 1024),
        cost_estimate=pl.CostEstimate(
            flops=flops,
            transcendentals=2 * query_rows * key_rows,
            bytes_accessed=key_rows * HD * 2 * 4,
        ),
    )(mask, queries, output_grad, attn_output, key_value)


def _pair_permute(value, distances):
    ctx_count, tp_count = lax.axis_size("ctx"), lax.axis_size("tp")
    pairs = [
        (c * tp_count + t, (c ^ distances[t % 2]) * tp_count + t)
        for c in range(ctx_count)
        for t in range(tp_count)
    ]
    return lax.ppermute(value, ("ctx", "tp"), pairs)


def gather_positions(me, distances, count):
    offset = me ^ jnp.arange(count, dtype=jnp.int32)
    return sum(((offset & d) != 0).astype(jnp.int32) << r for r, d in enumerate(distances))


def _coefficient_masks(distances):
    width = max(distances).bit_length()
    masks = []
    for r in range(len(distances)):
        for m in range(1 << width):
            if all(bin(d & m).count("1") % 2 == (r == s) for s, d in enumerate(distances)):
                masks.append(m)
                break
    return masks


def scatter_positions(me, distances, count):
    offset = me ^ jnp.arange(count, dtype=jnp.int32)
    top = len(distances) - 1
    return sum(
        ((lax.population_count(offset & m) & 1) == 0).astype(jnp.int32) << (top - r)
        for r, m in enumerate(_coefficient_masks(distances))
    )


def per_core(core, tables):
    return jnp.where(core == 0, tables[0], tables[1])


def concat_gather(x, orders):
    held = x
    for distances in zip(*orders):
        held = jnp.concatenate([held, _pair_permute(held, distances)], axis=0)
    return held


def halving_reduce(x, orders, wire=jnp.bfloat16):
    held = x
    for distances in zip(*orders):
        half = held.shape[0] // 2
        sent = _pair_permute(held[:half].astype(wire), distances)
        held = held[half:].astype(jnp.float32) + sent.astype(jnp.float32)
    return held


def tp_positions(me, core, count):
    first, rest = TP_ORDERS[0][0], [order[1:] for order in TP_ORDERS]
    assert all(order[0] == first for order in TP_ORDERS)
    offset = me ^ jnp.arange(count, dtype=jnp.int32)
    sent = (lax.population_count(offset & _coefficient_masks(TP_ORDERS[0])[0]) & 1) == 1

    def later(off, order):
        masks = _coefficient_masks((first,) + tuple(order))[1:]
        top = len(masks) - 1
        return sum(
            ((lax.population_count(off & m) & 1) == 0).astype(jnp.int32) << (top - r)
            for r, m in enumerate(masks)
        )

    mine = per_core(core, [later(offset, o) for o in rest])
    theirs = per_core(core, [later(offset ^ first, o) for o in reversed(rest)])
    return jnp.where(sent, theirs, count // 2 + mine)


def tp_halving_reduce(x, orders, wire=jnp.bfloat16):
    count = lax.axis_size("tp")
    held = x
    for distances in zip(*orders):
        half = held.shape[0] // 2
        pairs = [(i, i ^ distances[i % 2]) for i in range(count)]
        sent = lax.ppermute(held[:half].astype(wire), "tp", pairs)
        held = held[half:].astype(jnp.float32) + sent.astype(jnp.float32)
    return held


def xor_of_position(distances, count):
    position = jnp.arange(count, dtype=jnp.int32)
    return sum(((position >> r) & 1) * d for r, d in enumerate(distances))


def per_device(
    queries, key_states, value_states, attn_output, output_grad, block_map, w_query, w_key, w_value
):
    slab_rows, width = queries.shape
    ctx_count = lax.axis_size("ctx")
    me = lax.axis_index("ctx")
    tp_count = lax.axis_size("tp")
    me_tp = lax.axis_index("tp")
    core = me_tp % 2
    odd = me % 2
    low = odd == 0
    arrays = (queries, output_grad, attn_output, key_states, value_states)
    kept = jnp.concatenate([lax.dynamic_slice_in_dim(x, odd * HD, HD, 1) for x in arrays], axis=1)
    given = jnp.concatenate(
        [lax.dynamic_slice_in_dim(x, (1 - odd) * HD, HD, 1) for x in arrays], axis=1
    )
    got = _pair_permute(given, (1, 1))
    both = jnp.where(low, jnp.concatenate([kept, got], 0), jnp.concatenate([got, kept], 0))
    pair_q, pair_do, pair_o = both[:, 0:HD], both[:, HD : 2 * HD], both[:, 2 * HD : 3 * HD]
    pair_kv = both[:, 3 * HD : 5 * HD]
    gathered = concat_gather(pair_kv, HEAD_GATHER_ORDERS)
    group_count = ctx_count // 2
    holder = me ^ per_core(core, [xor_of_position(o, group_count) for o in HEAD_GATHER_ORDERS])
    base = holder - holder % 2
    key_slabs = jnp.stack([base, base + 1], axis=1).reshape(-1) * slab_rows // BLK
    first = (me - odd) * slab_rows // BLK
    mask_rows = jnp.stack([block_map[first][key_slabs], block_map[first + 1][key_slabs]])
    mask = jnp.repeat(mask_rows.astype(jnp.float32), BLK, axis=1)
    mask = jnp.concatenate([mask, jnp.zeros((6, mask.shape[1]), jnp.float32)], axis=0)
    pair_dq, part_grads = slab_attention(mask, pair_q, pair_do, pair_o, gathered, 2)
    finished = halving_reduce(part_grads, HEAD_SCATTER_ORDERS).astype(jnp.bfloat16)
    pair_grads = jnp.concatenate([pair_dq.astype(jnp.bfloat16), finished], axis=1)
    lower, upper = pair_grads[:slab_rows], pair_grads[slab_rows:]
    mine = jnp.where(low, lower, upper)
    back = _pair_permute(jnp.where(low, upper, lower), (1, 1))
    first_head = jnp.where(low, mine, back)
    second_head = jnp.where(low, back, mine)
    own_grads = jnp.concatenate(
        [
            first_head[:, 0:HD], second_head[:, 0:HD],
            first_head[:, HD : 2 * HD], second_head[:, HD : 2 * HD],
            first_head[:, 2 * HD : 3 * HD], second_head[:, 2 * HD : 3 * HD],
        ],
        axis=1,
    )
    gather_at = per_core(core, [gather_positions(me, o, ctx_count) for o in GATHER_ORDERS])
    held = concat_gather(own_grads, tuple(order[:-1] for order in GATHER_ORDERS))
    other = _pair_permute(held, tuple(order[-1] for order in GATHER_ORDERS))
    projections = jnp.concatenate([w_query, w_key, w_value], axis=1)

    def project(rows):
        return lax.dot_general(
            rows, projections, (((1,), (1,)), ((), ())), preferred_element_type=jnp.float32
        ).astype(jnp.bfloat16)

    term = jnp.concatenate([project(held), project(other)], axis=0)
    tp_at = tp_positions(me_tp, core, tp_count)
    owner = jnp.argsort(tp_at)
    per_owner = ctx_count // tp_count
    wanted = (owner[:, None] * per_owner + jnp.arange(per_owner)[None, :]).reshape(-1)
    source = gather_at[wanted]
    ordered = jnp.take(term.reshape(ctx_count, slab_rows, -1), source, axis=0)
    return tp_halving_reduce(ordered.reshape(ctx_count * slab_rows, -1), TP_ORDERS).astype(
        jnp.bfloat16
    )


def solution(mesh):
    return jax.shard_map(
        per_device,
        mesh=mesh,
        in_specs=(
            P("ctx", "tp"),
            P("ctx", "tp"),
            P("ctx", "tp"),
            P("ctx", "tp"),
            P("ctx", "tp"),
            P(),
            P("ctx", "tp"),
            P("ctx", "tp"),
            P("ctx", "tp"),
        ),
        out_specs=P("tp", "ctx"),
        check_vma=False,
    )
```

```python
import functools
import math

import jax
import jax.numpy as jnp
from jax import lax
from jax.experimental import pallas as pl
from jax.experimental.pallas import tpu as pltpu
from jax.sharding import PartitionSpec as P

HD = 128
BLK = 128


NEG_FILL = -1e30
GATHER_ORDERS = ((4, 2, 16, 8, 1), (4, 16, 2, 1, 8))
SCATTER_ORDERS = tuple(tuple(reversed(order)) for order in GATHER_ORDERS)
HEAD_GATHER_ORDERS = ((4, 8, 2, 16), (4, 8, 16, 2))
HEAD_SCATTER_ORDERS = tuple(tuple(reversed(order)) for order in HEAD_GATHER_ORDERS)
TP_ORDERS = ((1, 4, 12, 2), (1, 12, 4, 2))


def _nt(a, b):
    return lax.dot_general(a, b, (((1,), (1,)), ((), ())), preferred_element_type=jnp.float32)


def _tn(a, b):
    return lax.dot_general(a, b, (((0,), (0,)), ((), ())), preferred_element_type=jnp.float32)


def attention_kernel(slab_count, score_scale, mask_ref, q_ref, do_ref, o_ref, kv_ref, dq_ref, dkdv_ref):
    key_rows = kv_ref.shape[0]
    rows = q_ref.shape[0] // slab_count
    block = rows * slab_count
    block_count = key_rows // block
    k_h = kv_ref[:, 0:HD]
    dk_total = jnp.zeros((key_rows, HD), jnp.float32)
    dv_total = jnp.zeros((key_rows, HD), jnp.float32)
    for a in range(slab_count):
        mine = slice(a * rows, (a + 1) * rows)
        allowed = mask_ref[a : a + 1, :] > 0
        q_h = q_ref[mine, :]
        do_h = do_ref[mine, :]
        scores = _nt(q_h, k_h) * score_scale
        masked = jnp.where(allowed, scores, NEG_FILL)
        row_max = jnp.max(masked, axis=1, keepdims=True)
        row_sum = jnp.sum(jnp.where(allowed, jnp.exp(masked - row_max), 0.0), axis=1, keepdims=True)
        log_total = row_max + jnp.log(row_sum)
        probs = jnp.where(allowed, jnp.exp(masked - log_total), 0.0)
        row_delta = jnp.sum(
            do_h.astype(jnp.float32) * o_ref[mine, :].astype(jnp.float32), axis=1, keepdims=True
        )
        dprobs = _nt(do_h, kv_ref[:, HD : 2 * HD])
        score_gradient = (probs * (dprobs - row_delta) * score_scale).astype(jnp.bfloat16)
        dq_ref[mine, :] = jnp.dot(score_gradient, k_h, preferred_element_type=jnp.float32)
        dk_total = dk_total + _tn(score_gradient, q_h)
        dv_total = dv_total + _tn(probs.astype(jnp.bfloat16), do_h)
    dk = dk_total.astype(jnp.bfloat16)
    dv = dv_total.astype(jnp.bfloat16)
    for p in range(block_count):
        src = slice(p * block, (p + 1) * block)
        dst = slice((block_count - 1 - p) * block, (block_count - p) * block)
        dkdv_ref[dst, 0:HD] = dk[src]
        dkdv_ref[dst, HD : 2 * HD] = dv[src]


def slab_attention(mask, queries, output_grad, attn_output, key_value, slab_count):
    query_rows = queries.shape[0]
    key_rows = key_value.shape[0]
    vmem = pl.BlockSpec(memory_space=pltpu.VMEM)
    flops = 2 * query_rows * key_rows * HD * 5
    return pl.pallas_call(
        functools.partial(attention_kernel, slab_count, 1.0 / math.sqrt(HD)),
        out_shape=(
            jax.ShapeDtypeStruct((query_rows, HD), jnp.float32),
            jax.ShapeDtypeStruct((key_rows, 2 * HD), jnp.bfloat16),
        ),
        in_specs=[vmem] * 5,
        out_specs=(vmem, vmem),
        compiler_params=pltpu.CompilerParams(vmem_limit_bytes=48 * 1024 * 1024),
        cost_estimate=pl.CostEstimate(
            flops=flops,
            transcendentals=2 * query_rows * key_rows,
            bytes_accessed=key_rows * HD * 2 * 4,
        ),
    )(mask, queries, output_grad, attn_output, key_value)


def _pair_permute(value, distances):
    ctx_count, tp_count = lax.axis_size("ctx"), lax.axis_size("tp")
    pairs = [
        (c * tp_count + t, (c ^ distances[t % 2]) * tp_count + t)
        for c in range(ctx_count)
        for t in range(tp_count)
    ]
    return lax.ppermute(value, ("ctx", "tp"), pairs)


def gather_positions(me, distances, count):
    offset = me ^ jnp.arange(count, dtype=jnp.int32)
    return sum(((offset & d) != 0).astype(jnp.int32) << r for r, d in enumerate(distances))


def _coefficient_masks(distances):
    width = max(distances).bit_length()
    masks = []
    for r in range(len(distances)):
        for m in range(1 << width):
            if all(bin(d & m).count("1") % 2 == (r == s) for s, d in enumerate(distances)):
                masks.append(m)
                break
    return masks


def scatter_positions(me, distances, count):
    offset = me ^ jnp.arange(count, dtype=jnp.int32)
    top = len(distances) - 1
    return sum(
        ((lax.population_count(offset & m) & 1) == 0).astype(jnp.int32) << (top - r)
        for r, m in enumerate(_coefficient_masks(distances))
    )


def per_core(core, tables):
    return jnp.where(core == 0, tables[0], tables[1])


def concat_gather(x, orders):
    held = x
    for distances in zip(*orders):
        held = jnp.concatenate([held, _pair_permute(held, distances)], axis=0)
    return held


def halving_reduce(x, orders, wire=jnp.bfloat16):
    held = x
    for distances in zip(*orders):
        half = held.shape[0] // 2
        sent = _pair_permute(held[:half].astype(wire), distances)
        held = held[half:].astype(jnp.float32) + sent.astype(jnp.float32)
    return held


def tp_positions(me, core, count):
    first, rest = TP_ORDERS[0][0], [order[1:] for order in TP_ORDERS]
    assert all(order[0] == first for order in TP_ORDERS)
    offset = me ^ jnp.arange(count, dtype=jnp.int32)
    sent = (lax.population_count(offset & _coefficient_masks(TP_ORDERS[0])[0]) & 1) == 1

    def later(off, order):
        masks = _coefficient_masks((first,) + tuple(order))[1:]
        top = len(masks) - 1
        return sum(
            ((lax.population_count(off & m) & 1) == 0).astype(jnp.int32) << (top - r)
            for r, m in enumerate(masks)
        )

    mine = per_core(core, [later(offset, o) for o in rest])
    theirs = per_core(core, [later(offset ^ first, o) for o in reversed(rest)])
    return jnp.where(sent, theirs, count // 2 + mine)


def tp_halving_reduce(x, orders, wire=jnp.bfloat16):
    count = lax.axis_size("tp")
    held = x
    for distances in zip(*orders):
        half = held.shape[0] // 2
        pairs = [(i, i ^ distances[i % 2]) for i in range(count)]
        sent = lax.ppermute(held[:half].astype(wire), "tp", pairs)
        held = held[half:].astype(jnp.float32) + sent.astype(jnp.float32)
    return held


def xor_of_position(distances, count):
    position = jnp.arange(count, dtype=jnp.int32)
    return sum(((position >> r) & 1) * d for r, d in enumerate(distances))


def per_device(
    queries, key_states, value_states, attn_output, output_grad, block_map, w_query, w_key, w_value
):
    slab_rows, width = queries.shape
    ctx_count = lax.axis_size("ctx")
    me = lax.axis_index("ctx")
    tp_count = lax.axis_size("tp")
    me_tp = lax.axis_index("tp")
    core = me_tp % 2
    odd = me % 2
    low = odd == 0
    arrays = (queries, output_grad, attn_output, key_states, value_states)
    kept = jnp.concatenate([lax.dynamic_slice_in_dim(x, odd * HD, HD, 1) for x in arrays], axis=1)
    given = jnp.concatenate(
        [lax.dynamic_slice_in_dim(x, (1 - odd) * HD, HD, 1) for x in arrays], axis=1
    )
    got = _pair_permute(given, (1, 1))
    both = jnp.where(low, jnp.concatenate([kept, got], 0), jnp.concatenate([got, kept], 0))
    pair_q, pair_do, pair_o = both[:, 0:HD], both[:, HD : 2 * HD], both[:, 2 * HD : 3 * HD]
    pair_kv = both[:, 3 * HD : 5 * HD]
    gathered = concat_gather(pair_kv, HEAD_GATHER_ORDERS)
    group_count = ctx_count // 2
    holder = me ^ per_core(core, [xor_of_position(o, group_count) for o in HEAD_GATHER_ORDERS])
    base = holder - holder % 2
    key_slabs = jnp.stack([base, base + 1], axis=1).reshape(-1) * slab_rows // BLK
    first = (me - odd) * slab_rows // BLK
    mask_rows = jnp.stack([block_map[first][key_slabs], block_map[first + 1][key_slabs]])
    mask = jnp.repeat(mask_rows.astype(jnp.float32), BLK, axis=1)
    mask = jnp.concatenate([mask, jnp.zeros((6, mask.shape[1]), jnp.float32)], axis=0)
    pair_dq, part_grads = slab_attention(mask, pair_q, pair_do, pair_o, gathered, 2)
    finished = halving_reduce(part_grads, HEAD_SCATTER_ORDERS).astype(jnp.bfloat16)
    pair_grads = jnp.concatenate([pair_dq.astype(jnp.bfloat16), finished], axis=1)
    lower, upper = pair_grads[:slab_rows], pair_grads[slab_rows:]
    mine = jnp.where(low, lower, upper)
    back = _pair_permute(jnp.where(low, upper, lower), (1, 1))
    first_head = jnp.where(low, mine, back)
    second_head = jnp.where(low, back, mine)
    own_grads = jnp.concatenate(
        [
            first_head[:, 0:HD], second_head[:, 0:HD],
            first_head[:, HD : 2 * HD], second_head[:, HD : 2 * HD],
            first_head[:, 2 * HD : 3 * HD], second_head[:, 2 * HD : 3 * HD],
        ],
        axis=1,
    )
    gather_at = per_core(core, [gather_positions(me, o, ctx_count) for o in GATHER_ORDERS])
    held = concat_gather(own_grads, tuple(order[:-1] for order in GATHER_ORDERS))
    other = _pair_permute(held, tuple(order[-1] for order in GATHER_ORDERS))
    projections = jnp.concatenate([w_query, w_key, w_value], axis=1)

    def project(rows):
        return lax.dot_general(
            rows, projections, (((1,), (1,)), ((), ())), preferred_element_type=jnp.float32
        ).astype(jnp.bfloat16)

    term = jnp.concatenate([project(held), project(other)], axis=0)
    tp_at = tp_positions(me_tp, core, tp_count)
    owner = jnp.argsort(tp_at)
    per_owner = ctx_count // tp_count
    wanted = (owner[:, None] * per_owner + jnp.arange(per_owner)[None, :]).reshape(-1)
    source = gather_at[wanted]
    ordered = jnp.take(term.reshape(ctx_count, slab_rows, -1), source, axis=0)
    return tp_halving_reduce(ordered.reshape(ctx_count * slab_rows, -1), TP_ORDERS).astype(
        jnp.bfloat16
    )


def solution(mesh):
    return jax.shard_map(
        per_device,
        mesh=mesh,
        in_specs=(
            P("ctx", "tp"),
            P("ctx", "tp"),
            P("ctx", "tp"),
            P("ctx", "tp"),
            P("ctx", "tp"),
            P(),
            P("ctx", "tp"),
            P("ctx", "tp"),
            P("ctx", "tp"),
        ),
        out_specs=P("tp", "ctx"),
        check_vma=False,
    )
```
